256 devices in a mesh: grp: 8 (over y, core), row: 32 (over z, x).
Axes of the slice: x: 4, y: 4, z: 8, core: 2. Of those that a mesh axis runs over, the one named last changes fastest.
Arguments:
- fine_cols: int32 [10240, 5], P(('grp', 'row')), may hold values from 0 to 10239, as said below
- fine_blocks: bfloat16 [10240, 5, 128, 128], P(('grp', 'row'))
- prolong_cols: int32 [10240, 2], replicated, may hold values from 0 to 1023, as said below
- prolong_blocks: bfloat16 [10240, 2, 128, 128], P(('grp', 'row')), may hold values from -0.125 to 0.125
- agg_owner: int32 [1024], replicated, may hold values from 0 to 7, as said below
- coarse_rhs: float32 [1024, 128], P(('grp', 'row')), may hold values from -6 to 6
- lam_low: float32 [1], replicated, may hold values from 0.05 to 0.5
- lam_high: float32 [1], replicated, may hold values from 1.5 to 3.5
Outputs:
- coarse_operator: float32 [2048, 7, 128, 128], P(('grp', 'row'))
- coarse_solution: float32 [2048, 128], P(('grp', 'row'))
- coarse_residual: float32 [2048, 128], P(('grp', 'row'))
The draws below stay inside these ranges and needn't reach their ends.
Inputs may be any that keep to these rules, and one draw needn't show every extreme that they name: fine_cols[i, 0] = i; the other 4 entries of row i are distinct rows (i + t) mod 10240 with 1 <= |t| <= 10; some row reaches |t| = 10. `prolong_cols`: the two entries of fine row i are two distinct ones of i // 10 - 1, i // 10, i // 10 + 1 in rising order, taken modulo 1024. `agg_owner`: the 4 aggregates made on one device go to distinct groups; for every row index some group owns one aggregate from each of the 8 groups at that row index.
All inputs are finite; a program needn't handle non-finite values.
Results may differ from the reference program's by a relative error of at most 0.0019.
Values may be sent and summed in bfloat16 or wider, within the bound.
A program may use at most 128 MiB of HBM per device.

```python
import math
import jax
import jax.numpy as jnp
from jax import lax

BLK = 128
AGGS = 4
KA = 5
KP = 2
KC = 7
AGG = 10
NF = 10240
NC = 1024
SLOTS = 8
N_GRP = 8
N_ROW = 32


def draw_fine_cols(key, part):
    fine_rows = jnp.arange(NF, dtype=jnp.int32)
    candidates = jnp.concatenate([jnp.arange(-AGG, 0, dtype=jnp.int32), jnp.arange(1, AGG + 1, dtype=jnp.int32)])
    scores = jax.random.randint(key, (NF, 2 * AGG), 0, 1 << 20, dtype=jnp.int32) * (2 * AGG) + jnp.arange(2 * AGG, dtype=jnp.int32)
    forced = ((fine_rows[:, None] == 0) & (jnp.abs(candidates)[None, :] == AGG)).astype(jnp.int32)
    scores = scores + forced * (1 << 26)
    top_scores, picked = lax.top_k(scores, KA - 1)
    steps_away = jnp.take(candidates, picked)
    reach = jnp.concatenate([jnp.zeros((NF, 1), jnp.int32), steps_away], axis=1)
    return (fine_rows[:, None] + reach) % NF


def draw_prolong_cols(key, part):
    fine_rows = jnp.arange(NF, dtype=jnp.int32)
    dropped = jax.random.randint(key, (NF,), 0, 3, dtype=jnp.int32)
    home = fine_rows // AGG
    lower = home - 1 + (dropped == 0).astype(jnp.int32)
    upper = home + 1 - (dropped == 2).astype(jnp.int32)
    return jnp.stack([lower, upper], axis=1) % NC


def draw_agg_owner(key, part):
    devices = N_GRP * N_ROW
    full_group = jax.random.randint(jax.random.fold_in(key, 1), (N_ROW,), 0, N_GRP, dtype=jnp.int32)
    device_ids = jnp.arange(devices, dtype=jnp.int32)
    full_here = full_group[device_ids % N_ROW]
    scores = jax.random.randint(jax.random.fold_in(key, 2), (devices, N_GRP), 0, 1 << 20, dtype=jnp.int32) * N_GRP + jnp.arange(N_GRP, dtype=jnp.int32)
    scores = scores + (jnp.arange(N_GRP, dtype=jnp.int32)[None, :] == full_here[:, None]).astype(jnp.int32) * (1 << 26)
    top_scores, groups = lax.top_k(scores, AGGS)
    order = jax.random.randint(jax.random.fold_in(key, 3), (devices, AGGS), 0, 1 << 20, dtype=jnp.int32) * AGGS + jnp.arange(AGGS, dtype=jnp.int32)
    order_scores, shuffle = lax.top_k(order, AGGS)
    owners = jnp.take_along_axis(groups, shuffle, axis=1)
    return owners.reshape(-1)


def draw_fine_blocks(key, part):
    spread = 0.006
    noise = spread * jax.random.normal(key, (NF, KA, BLK, BLK), jnp.float32)
    identity = jnp.eye(BLK, dtype=jnp.float32)
    diagonal_slot = (jnp.arange(KA) == 0).astype(jnp.float32)
    blocks = noise + diagonal_slot[None, :, None, None] * identity[None, None, :, :]
    return blocks.astype(jnp.bfloat16)


def level_of(stream_key, extent, cuts, smallest, high):
    loudness = 1.0
    for dim, parts in cuts:
        heights = jax.random.uniform(jax.random.fold_in(jax.random.fold_in(stream_key, 6), dim), (parts,), jnp.float32, smallest / len(cuts), high / len(cuts))
        loudness = loudness * jnp.repeat(jnp.exp(heights), extent[dim] // parts).reshape((-1,) + (1,) * (len(extent) - 1 - dim))
    return loudness


def centred(own_key, shape, scale, limit, cuts=(), held_as=jnp.bfloat16):
    drawn = jax.random.normal(own_key, shape, jnp.float32) * scale
    if len(cuts) > 0:
        drawn = level_of(own_key, shape, cuts, -0.22, 0.18) * drawn
    return jnp.clip(drawn, min=-limit, max=limit).astype(held_as)


def setup_inputs(seed: int = 0) -> dict:
    splits = jax.random.split(jax.random.key(seed), 9)
    return {
        "fine_cols": draw_fine_cols(jax.random.fold_in(splits[8], 71), 0),
        "fine_blocks": draw_fine_blocks(jax.random.fold_in(splits[8], 71), 0),
        "prolong_cols": draw_prolong_cols(jax.random.fold_in(splits[8], 71), 0),
        "prolong_blocks": centred(splits[3], (NF, KP, BLK, BLK), (2 * AGG * BLK) ** -0.5, 0.125, ((0, 256),)),
        "agg_owner": draw_agg_owner(jax.random.fold_in(splits[8], 71), 0),
        "coarse_rhs": centred(splits[5], (NC, BLK), 1.0, 6.0, ((0, 256),), jnp.float32),
        "lam_low": jnp.clip(jnp.exp(jax.random.uniform(splits[6], (1,), jnp.float32, math.log(0.05), math.log(0.5))), 0.05, 0.5),
        "lam_high": jnp.clip(jax.random.uniform(splits[7], (1,), jnp.float32, 1.5, 3.5), 1.5, 3.5),
    }


HIGH = lax.Precision.HIGHEST


def chebyshev_terms(lam_low, lam_high):
    center = 0.5 * (lam_high[0] + lam_low[0])
    radius = 0.5 * (lam_high[0] - lam_low[0])
    sigma_ratio = center / radius
    first_rho = 1.0 / sigma_ratio
    second_rho = 1.0 / (2.0 * sigma_ratio - first_rho)
    return center, second_rho * first_rho, 2.0 * second_rho / radius


def reference(fine_cols, fine_blocks, prolong_cols, prolong_blocks, agg_owner, coarse_rhs, lam_low, lam_high):
    offsets = jnp.arange(-2, 3, dtype=jnp.int32)

    def one_aggregate(agg_id):
        start = agg_id * AGG
        block_a = lax.dynamic_slice_in_dim(fine_blocks, start, AGG, 0).astype(jnp.float32)
        cols_here = lax.dynamic_slice_in_dim(fine_cols, start, AGG, 0)
        p_near = jnp.take(prolong_blocks, cols_here, axis=0).astype(jnp.float32)
        near_cols = jnp.take(prolong_cols, cols_here, axis=0)
        shifted = (near_cols - agg_id + 2) % NC - 2
        chosen = (shifted[..., None] == offsets).astype(jnp.float32)
        products = jnp.einsum("iakm,iaqmn->iaqkn", block_a, p_near, precision=HIGH)
        summed = jnp.einsum("iaqo,iaqkn->iokn", chosen, products, precision=HIGH)
        merged = lax.optimization_barrier(summed.astype(jnp.bfloat16)).astype(jnp.float32)
        own_blocks = lax.dynamic_slice_in_dim(prolong_blocks, start, AGG, 0).astype(jnp.float32)
        own_cols = lax.dynamic_slice_in_dim(prolong_cols, start, AGG, 0)
        step_off = (own_cols - agg_id + 1) % NC - 1
        term_blocks = jnp.einsum("ipmk,iomn->ipokn", own_blocks, merged, precision=HIGH)
        lifted = step_off[:, :, None, None, None]
        placing = ((lifted + 1 == jnp.arange(3, dtype=jnp.int32)[:, None])
                   & (offsets[None, None, :, None, None] - lifted + 3 == jnp.arange(KC, dtype=jnp.int32))).astype(jnp.float32)
        return jnp.einsum("ipots,ipokn->tskn", placing, term_blocks, precision=HIGH)

    pieces = lax.map(one_aggregate, jnp.arange(NC, dtype=jnp.int32))
    coarse = jnp.roll(pieces[:, 0], -1, axis=0) + pieces[:, 1] + jnp.roll(pieces[:, 2], 1, axis=0)
    cols_band = (jnp.arange(NC, dtype=jnp.int32)[:, None] + jnp.arange(KC, dtype=jnp.int32) - 3) % NC

    def operate(vector):
        nearby = jnp.take(vector, cols_band, axis=0)
        return jnp.einsum("csmn,csn->cm", coarse, nearby, precision=HIGH)

    center, old_weight, resid_weight = chebyshev_terms(lam_low, lam_high)
    first_iter = coarse_rhs / center
    first_resid = coarse_rhs - operate(first_iter)
    second_iter = first_iter + old_weight * first_iter + resid_weight * first_resid
    second_resid = coarse_rhs - operate(second_iter)
    coarse_ids = jnp.arange(NC, dtype=jnp.int32)
    native_dev = coarse_ids // AGGS
    grp_id = native_dev // N_ROW
    row_id = native_dev % N_ROW
    place_at = (agg_owner * N_ROW + row_id) * N_GRP + grp_id
    total_slots = N_GRP * N_ROW * SLOTS
    out_operator = jnp.zeros((total_slots, KC, BLK, BLK), jnp.float32).at[place_at].set(coarse)
    out_solution = jnp.zeros((total_slots, BLK), jnp.float32).at[place_at].set(second_iter)
    out_residual = jnp.zeros((total_slots, BLK), jnp.float32).at[place_at].set(second_resid)
    return (out_operator, out_solution, out_residual)
```

```python
import functools

import jax
import jax.numpy as jnp
from jax import lax
from jax.experimental import pallas as pl
from jax.experimental.pallas import tpu as pltpu
from jax.sharding import PartitionSpec as P

MESH = pl.DeviceIdType.MESH
BLK = 128
AGG = 10
AGGS = 4
ROWS = AGG * AGGS
F32 = jnp.float32
BF16 = jnp.bfloat16
Q_MAX = 32767.0
TINY = 2.0**-110


def chebyshev_terms(lam_low, lam_high):
    center = 0.5 * (lam_high[0] + lam_low[0])
    radius = 0.5 * (lam_high[0] - lam_low[0])
    sigma_ratio = center / radius
    first_rho = 1.0 / sigma_ratio
    second_rho = 1.0 / (2.0 * sigma_ratio - first_rho)
    return (center, second_rho * first_rho, 2.0 * second_rho / radius)


def quantised(block):
    top = jnp.maximum(jnp.max(jnp.abs(block), axis=0, keepdims=True), TINY)
    q = jnp.floor(block * (Q_MAX / top) + 0.5).astype(jnp.int32).astype(jnp.int16)
    return q, top * (1.0 / Q_MAX)


def kernel(
    groups, rows_axis,
    tbl, sel, par, a_hbm, p_hbm, rhs_ref,
    q_out, sc_out, xr_out,
    a_v, p_v, h_lo, h_hi, pt, m_v, acc_lo, acc_hi, co, qb, sb, sq, ss, xrb, sx,
    pq_s, ps_s, pq_r, ps_r, own, halo_x, own2, halo_x2,
    a_sem, p_sem, nb_send, nb_recv, gq_send, gq_recv, gs_send, gs_recv, gx_send, gx_recv, self_sem,
):
    g = lax.axis_index("grp")
    r = lax.axis_index("row")
    last = (r + 1) // rows_axis
    nxt = ((g + last) % groups, (r + 1) % rows_axis)
    first = (rows_axis - r) // rows_axis
    prv = ((g + groups - first) % groups, (r + rows_axis - 1) % rows_axis)

    a_copies = [
        pltpu.make_async_copy(a_hbm.at[pl.ds(k * AGG, AGG)], a_v.at[pl.ds(k * AGG, AGG)], a_sem.at[k])
        for k in range(AGGS)
    ]
    p_copy = pltpu.make_async_copy(p_hbm, p_v.at[pl.ds(0, 2 * ROWS)], p_sem)
    p_copy.start()
    for k in (1, 2, 0, 3):
        a_copies[k].start()

    zero_block = jnp.zeros((BLK, BLK), BF16)
    p_v[2 * ROWS] = zero_block
    h_lo[2 * AGG] = zero_block
    h_hi[2 * AGG] = zero_block
    own[...] = jnp.zeros_like(own)
    own[0:AGGS, :] = rhs_ref[...]

    barrier = pltpu.get_barrier_semaphore()
    for target in (nxt, prv):
        pl.semaphore_signal(barrier, inc=1, device_id=target, device_id_type=MESH)
    for off in range(1, groups):
        pl.semaphore_signal(barrier, inc=1, device_id=((g + off) % groups, r), device_id_type=MESH)
    pl.semaphore_wait(barrier, groups + 1)

    def to_neighbour(slot, src, dst, target):
        return pltpu.make_async_remote_copy(
            src_ref=src, dst_ref=dst, send_sem=nb_send.at[slot], recv_sem=nb_recv.at[slot],
            device_id=target, device_id_type=MESH)

    p_next = to_neighbour(0, p_hbm.at[pl.ds(2 * (ROWS - AGG), 2 * AGG)], h_lo.at[pl.ds(0, 2 * AGG)], nxt)
    p_prev = to_neighbour(1, p_hbm.at[pl.ds(0, 2 * AGG)], h_hi.at[pl.ds(0, 2 * AGG)], prv)
    p_next.start()
    p_prev.start()
    x_next = to_neighbour(2, own, halo_x.at[0], nxt)
    x_prev = to_neighbour(3, own, halo_x.at[1], prv)
    x_next.start()
    x_prev.start()

    co[...] = jnp.zeros_like(co)
    p_copy.wait()

    def turn(i, carry):
        for t in range(3):
            pt[i, t * BLK:(t + 1) * BLK, :] = p_v[tbl[i, 25 + t]].T
        return carry

    lax.fori_loop(0, ROWS, turn, 0)

    def gathered(ref, i, first_col, stride, aa, cols):
        return jnp.concatenate(
            [jnp.concatenate([ref[tbl[i, first_col + a * stride + o]] for o in cols], axis=1) for a in range(aa)],
            axis=0)

    def local_rows(start, count, plan):
        def step(n, carry):
            i = start + n
            lhs = jnp.concatenate([a_v[i, a] for a in range(5)], axis=1)
            for cols, keep, base in plan:
                got = jnp.dot(lhs, gathered(p_v, i, 0, 5, 5, cols), preferred_element_type=F32)
                lo = (cols[0] - base) * BLK
                hi = (cols[-1] + 1 - base) * BLK
                if keep is None:
                    m_v[i, :, lo:hi] = got.astype(BF16)
                else:
                    keep[n, :, lo:hi] = got
            return carry

        lax.fori_loop(0, count, step, 0)

    a_copies[1].wait()
    a_copies[2].wait()
    local_rows(AGG, 2 * AGG, (((0, 1), None, 0), ((2, 3), None, 0), ((4,), None, 0)))
    a_copies[0].wait()
    local_rows(0, AGG, (((0, 1), acc_lo, 0), ((2,), acc_lo, 0), ((3, 4), None, 0)))
    a_copies[3].wait()
    local_rows(3 * AGG, AGG, (((0, 1), None, 0), ((2, 3), acc_hi, 2), ((4,), acc_hi, 2)))

    def lift(k):
        lhs = jnp.concatenate([pt[k * AGG + n] for n in range(AGG)], axis=1)
        for cols in ((0, 1), (2, 3), (4,)):
            rhs = m_v[k * AGG:(k + 1) * AGG, :, cols[0] * BLK:(cols[-1] + 1) * BLK]
            rhs = rhs.reshape(AGG * BLK, len(cols) * BLK)
            got = jnp.dot(lhs, rhs, preferred_element_type=F32)
            for t in range(3):
                for n, o in enumerate(cols):
                    co[k + t, o - t + 2] += got[t * BLK:(t + 1) * BLK, n * BLK:(n + 1) * BLK]

    lift(1)
    lift(2)

    def halo_rows(start, ref, keep, base):
        def step(n, carry):
            i = start + n
            lhs = jnp.concatenate([a_v[i, a] for a in range(1, 5)], axis=1)
            for cols in ((0, 1), (2,)):
                got = jnp.dot(lhs, gathered(ref, i, 28, 3, 4, cols), preferred_element_type=F32)
                lo = cols[0] * BLK
                hi = (cols[-1] + 1) * BLK
                m_v[i, :, base * BLK + lo:base * BLK + hi] = (keep[n, :, lo:hi] + got).astype(BF16)
            return carry

        lax.fori_loop(0, AGG, step, 0)

    def send_partial(side, row, first_s, target, slot):
        ps_s[side] = jnp.zeros_like(ps_s[side])
        for n in range(5):
            q, scale = quantised(co[row, first_s + n])
            pq_s[side, n] = q
            ps_s[side, n:n + 1, :] = scale
        blocks = to_neighbour(slot, pq_s.at[side], pq_r.at[side], target)
        scales = to_neighbour(slot + 1, ps_s.at[side], ps_r.at[side], target)
        blocks.start()
        scales.start()
        return blocks, scales

    p_next.wait_recv()
    halo_rows(0, h_lo, acc_lo, 0)
    lift(0)
    sent_prev = send_partial(0, 0, 2, prv, 4)
    p_prev.wait_recv()
    halo_rows(3 * AGG, h_hi, acc_hi, 2)
    lift(3)
    sent_next = send_partial(1, 5, 0, nxt, 6)

    def pack(k):
        sb[k] = jnp.zeros_like(sb[k])
        for s in range(7):
            q, scale = quantised(co[k + 1, s])
            qb[k, s] = q
            sb[k, s:s + 1, :] = scale

    qb[AGGS] = jnp.zeros_like(qb[AGGS])
    sb[AGGS] = jnp.zeros_like(sb[AGGS])
    pack(1)
    pack(2)
    for copy in sent_prev:
        copy.wait_recv()
    for n in range(5):
        co[4, 2 + n] += pq_r[0, n].astype(jnp.int32).astype(F32) * ps_r[0, n:n + 1, :]
    pack(3)
    for copy in sent_next:
        copy.wait_recv()
    for n in range(5):
        co[1, n] += pq_r[1, n].astype(jnp.int32).astype(F32) * ps_r[1, n:n + 1, :]
    pack(0)

    def to_owner(off, src, dst, send, recv):
        return pltpu.make_async_remote_copy(
            src_ref=src.at[off], dst_ref=dst.at[g], send_sem=send.at[off], recv_sem=recv.at[off],
            device_id=((g + off) % groups, r), device_id_type=MESH)

    def from_maker(off, src, dst, send, recv):
        return pltpu.make_async_remote_copy(
            src_ref=src.at[off], dst_ref=dst.at[(g + groups - off) % groups], send_sem=send.at[off],
            recv_sem=recv.at[off], device_id=((g + groups - off) % groups, r), device_id_type=MESH)

    order = (4, 3, 5, 2, 6, 1, 7)
    for off in order + (0,):
        k = sel[(g + off) % groups]
        sq[off] = qb[k]
        ss[off] = sb[k]
        if off:
            to_owner(off, sq, q_out, gq_send, gq_recv).start()
            to_owner(off, ss, sc_out, gs_send, gs_recv).start()
    own_q = pltpu.make_async_copy(sq.at[0], q_out.at[g], self_sem.at[0])
    own_s = pltpu.make_async_copy(ss.at[0], sc_out.at[g], self_sem.at[1])
    own_q.start()
    own_s.start()

    x_next.wait_recv()
    x_prev.wait_recv()

    def applied(k, mine, halo, scale_by):
        total = None
        for s in range(7):
            c = k + s - 3
            if c < 0:
                row = halo[0, AGGS + c:AGGS + c + 1, :]
            elif c < AGGS:
                row = mine[c:c + 1, :]
            else:
                row = halo[1, c - AGGS:c - AGGS + 1, :]
            if scale_by is not None:
                row = row / scale_by
            term = co[k + 1, s] * row
            total = term if total is None else total + term
        return jnp.sum(total.T, axis=0, keepdims=True)

    center, old_weight, resid_weight = par[0], par[1], par[2]
    own2[...] = jnp.zeros_like(own2)
    for k in range(AGGS):
        rhs = own[k:k + 1, :]
        x1 = rhs / center
        own2[k:k + 1, :] = x1 + old_weight * x1 + resid_weight * (rhs - applied(k, own, halo_x, center))
    x2_next = to_neighbour(8, own2, halo_x2.at[0], nxt)
    x2_prev = to_neighbour(9, own2, halo_x2.at[1], prv)
    x2_next.start()
    x2_prev.start()
    xrb[...] = jnp.zeros_like(xrb)
    x2_next.wait_recv()
    x2_prev.wait_recv()
    for k in range(AGGS):
        xrb[k, 0:1, :] = own2[k:k + 1, :]
        xrb[k, 1:2, :] = own[k:k + 1, :] - applied(k, own2, halo_x2, None)
    for off in order + (0,):
        sx[off] = xrb[sel[(g + off) % groups]]
        if off:
            to_owner(off, sx, xr_out, gx_send, gx_recv).start()
    own_x = pltpu.make_async_copy(sx.at[0], xr_out.at[g], self_sem.at[2])
    own_x.start()

    for copy in (p_next, p_prev, x_next, x_prev, *sent_prev, *sent_next, x2_next, x2_prev):
        copy.wait_send()
    for off in order:
        for args in ((sq, q_out, gq_send, gq_recv), (ss, sc_out, gs_send, gs_recv), (sx, xr_out, gx_send, gx_recv)):
            to_owner(off, *args).wait_send()
            from_maker(off, *args).wait_recv()
    own_q.wait()
    own_s.wait()
    own_x.wait()


def call_kernel(groups, rows_axis, tbl, sel, par, a, p, rhs):
    hbm = pl.BlockSpec(memory_space=pl.ANY)
    smem = pl.BlockSpec(memory_space=pltpu.SMEM)
    vmem = pl.BlockSpec(memory_space=pltpu.VMEM)
    dma = pltpu.SemaphoreType.DMA
    i16 = jnp.int16
    return pl.pallas_call(
        functools.partial(kernel, groups, rows_axis),
        out_shape=(
            jax.ShapeDtypeStruct((groups, 7, BLK, BLK), i16),
            jax.ShapeDtypeStruct((groups, 8, BLK), F32),
            jax.ShapeDtypeStruct((groups, 8, BLK), F32),
        ),
        in_specs=[smem, smem, smem, hbm, hbm, vmem],
        out_specs=(hbm, hbm, hbm),
        scratch_shapes=[
            pltpu.VMEM((ROWS, 5, BLK, BLK), BF16),
            pltpu.VMEM((2 * ROWS + 1, BLK, BLK), BF16),
            pltpu.VMEM((2 * AGG + 1, BLK, BLK), BF16),
            pltpu.VMEM((2 * AGG + 1, BLK, BLK), BF16),
            pltpu.VMEM((ROWS, 3 * BLK, BLK), BF16),
            pltpu.VMEM((ROWS, BLK, 5 * BLK), BF16),
            pltpu.VMEM((AGG, BLK, 3 * BLK), F32),
            pltpu.VMEM((AGG, BLK, 3 * BLK), F32),
            pltpu.VMEM((AGGS + 2, 7, BLK, BLK), F32),
            pltpu.VMEM((AGGS + 1, 7, BLK, BLK), i16),
            pltpu.VMEM((AGGS + 1, 8, BLK), F32),
            pltpu.VMEM((groups, 7, BLK, BLK), i16),
            pltpu.VMEM((groups, 8, BLK), F32),
            pltpu.VMEM((AGGS + 1, 8, BLK), F32),
            pltpu.VMEM((groups, 8, BLK), F32),
            pltpu.VMEM((2, 5, BLK, BLK), i16),
            pltpu.VMEM((2, 8, BLK), F32),
            pltpu.VMEM((2, 5, BLK, BLK), i16),
            pltpu.VMEM((2, 8, BLK), F32),
            pltpu.VMEM((8, BLK), F32),
            pltpu.VMEM((2, 8, BLK), F32),
            pltpu.VMEM((8, BLK), F32),
            pltpu.VMEM((2, 8, BLK), F32),
            dma((AGGS,)), dma, dma((10,)), dma((10,)),
            dma((groups,)), dma((groups,)), dma((groups,)), dma((groups,)), dma((groups,)), dma((groups,)),
            dma((3,)),
        ],
        compiler_params=pltpu.CompilerParams(
            collective_id=0, has_side_effects=True, vmem_limit_bytes=56 << 20),
    )(tbl, sel, par, a, p, rhs)


def tables(fine_cols, prolong_cols, agg_owner, device, devices, groups):
    fine_total = ROWS * devices
    coarse_total = AGGS * devices
    first_row = device * ROWS
    base = device * AGGS
    pieces = [
        lax.dynamic_slice_in_dim(prolong_cols, (first_row - AGG) % fine_total, AGG, 0),
        lax.dynamic_slice_in_dim(prolong_cols, first_row, ROWS, 0),
        lax.dynamic_slice_in_dim(prolong_cols, (first_row + ROWS) % fine_total, AGG, 0),
    ]
    cols_pad = (jnp.concatenate(pieces, axis=0) - base + 8) % coarse_total - 8
    local = jnp.arange(ROWS, dtype=jnp.int32)
    reach = (fine_cols - (first_row + local)[:, None] + AGG) % fine_total - AGG
    where = local[:, None] + AGG + reach
    hit = where[:, :, None] == jnp.arange(ROWS + 2 * AGG, dtype=jnp.int32)
    near = jnp.sum(jnp.where(hit[..., None], cols_pad[None, None], 0), axis=2)
    offset = near - (local // AGG)[:, None, None] + 2
    match = offset[:, :, None, :] == jnp.arange(5, dtype=jnp.int32)[:, None]
    block = 2 * where[:, :, None] + jnp.arange(2, dtype=jnp.int32)
    inside = (where >= AGG) & (where < ROWS + AGG)

    def table(ok, shift, none):
        picked = jnp.where(match & ok[:, :, None, None], block[:, :, None, :] - shift - none, 0)
        return jnp.sum(picked, axis=3) + none

    here = table(inside, 2 * AGG, 2 * ROWS)
    below = table(where < AGG, 0, 2 * AGG)[:, 1:, 0:3]
    above = table(where >= ROWS + AGG, 2 * (ROWS + AGG), 2 * AGG)[:, 1:, 2:5]
    halo = jnp.where((local < 2 * AGG)[:, None, None], below, above)
    own = cols_pad[AGG:ROWS + AGG] - (local // AGG)[:, None] + 1
    own_match = own[:, None, :] == jnp.arange(3, dtype=jnp.int32)[:, None]
    own_block = (2 * local)[:, None] + jnp.arange(2, dtype=jnp.int32)
    mine = jnp.sum(jnp.where(own_match, own_block[:, None, :] - 2 * ROWS, 0), axis=2) + 2 * ROWS
    tbl = jnp.concatenate([here.reshape(ROWS, 25), mine, halo.reshape(ROWS, 12)], axis=1)
    owners = lax.dynamic_slice_in_dim(agg_owner, base, AGGS, 0)
    ids = jnp.arange(AGGS, dtype=jnp.int32)
    owned = owners[:, None] == jnp.arange(groups, dtype=jnp.int32)
    sel = jnp.sum(jnp.where(owned, (ids - AGGS)[:, None], 0), axis=0) + AGGS
    return tbl, sel


def per_device(
    fine_cols, fine_blocks, prolong_cols, prolong_blocks, agg_owner, coarse_rhs, lam_low, lam_high
):
    groups = lax.axis_size("grp")
    rows_axis = lax.axis_size("row")
    device = lax.axis_index("grp") * rows_axis + lax.axis_index("row")
    tbl, sel = tables(fine_cols, prolong_cols, agg_owner, device, groups * rows_axis, groups)
    par = jnp.stack(chebyshev_terms(lam_low, lam_high))
    q, scale, xr = call_kernel(
        groups, rows_axis, tbl, sel, par, fine_blocks, prolong_blocks.reshape(2 * ROWS, BLK, BLK), coarse_rhs)
    operator = q.astype(F32) * scale[:, :7, None, :]
    return operator, xr[:, 0], xr[:, 1]


def solution(mesh):
    return jax.shard_map(
        per_device,
        mesh=mesh,
        in_specs=(
            P(("grp", "row"), None),
            P(("grp", "row"), None, None, None),
            P(),
            P(("grp", "row"), None, None, None),
            P(),
            P(("grp", "row"), None),
            P(),
            P(),
        ),
        out_specs=(
            P(("grp", "row"), None, None, None),
            P(("grp", "row"), None),
            P(("grp", "row"), None),
        ),
        check_vma=False,
    )
```

```python
import functools

import jax
import jax.numpy as jnp
from jax import lax
from jax.experimental import pallas as pl
from jax.experimental.pallas import tpu as pltpu
from jax.sharding import PartitionSpec as P

MESH = pl.DeviceIdType.MESH
BLK = 128
AGG = 10
AGGS = 4
ROWS = AGG * AGGS
F32 = jnp.float32
BF16 = jnp.bfloat16
Q_MAX = 32767.0
TINY = 2.0**-110
SHIFT = (5, 3, 0, 0)
EARLY = 2


def quantised(block):
    top = jnp.maximum(jnp.max(jnp.abs(block), axis=0, keepdims=True), TINY)
    q = jnp.floor(block * (Q_MAX / top) + 0.5).astype(jnp.int32).astype(jnp.int16)
    return q, top * (1.0 / Q_MAX)


def chebyshev_terms(low, high):
    center = 0.5 * (high + low)
    radius = 0.5 * (high - low)
    sigma_ratio = center / radius
    first_rho = 1.0 / sigma_ratio
    second_rho = 1.0 / (2.0 * sigma_ratio - first_rho)
    return center, second_rho * first_rho, 2.0 * second_rho / radius


def wrapped(x, total):
    x = jnp.where(x > total // 2, x - total, x)
    return jnp.where(x < -(total // 2), x + total, x)


def write_tables(fine_total, coarse_total, first_row, base, fc, pc, tbl):
    row = lax.broadcasted_iota(jnp.int32, (5, ROWS), 1)
    reach = wrapped(fc[...] - (first_row + row), fine_total)
    place = row + AGG + reach
    near = [jnp.zeros((5, ROWS), jnp.int32) for _ in range(2)]
    start = (first_row + fine_total - AGG) % fine_total
    for p in range(ROWS + 2 * AGG):
        at = (start + p) % fine_total
        for q in range(2):
            near[q] = jnp.where(place == p, pc[q, at], near[q])
    agg = jnp.zeros((5, ROWS), jnp.int32)
    for k in range(1, AGGS):
        agg = agg + jnp.where(row >= k * AGG, 1, 0)
    offset = [wrapped(c - base - agg, coarse_total) + 2 for c in near]

    def pick(o, ok, block, none):
        got = jnp.where(ok & (offset[0] == o), block, none)
        return jnp.where(ok & (offset[1] == o), block + 1, got)

    inside = (place >= AGG) & (place < ROWS + AGG)
    for o in range(5):
        tbl[o, 0:5, 0:ROWS] = pick(o, inside, 2 * (place - AGG), 2 * ROWS)
    for o in range(3):
        below = pick(o, (place >= 0) & (place < AGG), 2 * place, 2 * AGG)
        above = pick(
            o + 2, (place >= ROWS + AGG) & (place < ROWS + 2 * AGG), 2 * (place - ROWS - AGG), 2 * AGG)
        tbl[5 + o, 0:5, 0:ROWS] = jnp.where(row < 2 * AGG, below, above)
    everywhere = row >= 0
    for t in range(3):
        tbl[8 + t, 0:5, 0:ROWS] = pick(t + 1, everywhere, 2 * row, 2 * ROWS)


def kernel(
    groups, rows_axis,
    pc, owner, lam_low, lam_high, fc, a_hbm, p_hbm, rhs_ref,
    q_out, sc_out, xr_out,
    tbl_v, tbl, a_v, p_v, h_lo, h_hi, pt, m_v, acc_lo, acc_hi, co, qb, sb, sq, ss, xrb, sx,
    pq_s, ps_s, pq_r, ps_r, own, halo_x, own2, halo_x2,
    a_sem, p_sem, t_sem, nb_send, nb_recv, ge_send, ge_recv, gq_send, gq_recv, gs_send, gs_recv, gx_send, gx_recv,
    self_sem,
):
    g = lax.axis_index("grp")
    r = lax.axis_index("row")
    device = g * rows_axis + r
    devices = groups * rows_axis
    base = device * AGGS
    last = (r + 1) // rows_axis
    nxt = ((g + last) % groups, (r + 1) % rows_axis)
    first = (rows_axis - r) // rows_axis
    prv = ((g + groups - first) % groups, (r + rows_axis - 1) % rows_axis)

    barrier = pltpu.get_barrier_semaphore()
    for target in (nxt, prv):
        pl.semaphore_signal(barrier, inc=1, device_id=target, device_id_type=MESH)
    for off in range(1, groups):
        pl.semaphore_signal(barrier, inc=1, device_id=((g + off) % groups, r), device_id_type=MESH)

    p_copy = pltpu.make_async_copy(p_hbm, p_v.at[pl.ds(0, 2 * ROWS)], p_sem)
    p_copy.start()
    a_copies = [
        pltpu.make_async_copy(a_hbm.at[pl.ds(k * AGG, AGG)], a_v.at[pl.ds(k * AGG, AGG)], a_sem.at[k])
        for k in range(AGGS)
    ]
    for k in (0, 1, 2, 3):
        a_copies[k].start()

    own[...] = jnp.zeros_like(own)
    own[0:AGGS, :] = rhs_ref[...]
    tbl_v[...] = jnp.zeros_like(tbl_v)
    write_tables(ROWS * devices, AGGS * devices, device * ROWS, base, fc, pc, tbl_v)
    t_copy = pltpu.make_async_copy(tbl_v, tbl, t_sem)
    t_copy.start()

    pl.semaphore_wait(barrier, groups + 1)

    def to_neighbour(slot, src, dst, target):
        return pltpu.make_async_remote_copy(
            src_ref=src, dst_ref=dst, send_sem=nb_send.at[slot], recv_sem=nb_recv.at[slot],
            device_id=target, device_id_type=MESH)

    p_next = to_neighbour(0, p_hbm.at[pl.ds(2 * (ROWS - AGG), 2 * AGG)], h_lo.at[pl.ds(0, 2 * AGG)], nxt)
    p_prev = to_neighbour(1, p_hbm.at[pl.ds(0, 2 * AGG)], h_hi.at[pl.ds(0, 2 * AGG)], prv)
    p_next.start()
    p_prev.start()
    x_next = to_neighbour(2, own, halo_x.at[0], nxt)
    x_prev = to_neighbour(3, own, halo_x.at[1], prv)
    x_next.start()
    x_prev.start()

    zero_block = jnp.zeros((BLK, BLK), BF16)
    p_v[2 * ROWS] = zero_block
    h_lo[2 * AGG] = zero_block
    h_hi[2 * AGG] = zero_block
    co[...] = jnp.zeros_like(co)
    t_copy.wait()
    p_copy.wait()

    def turn(i, carry):
        for t in range(3):
            pt[i, t * BLK:(t + 1) * BLK, :] = p_v[tbl[8 + t, 0, i]].T
        return carry

    lax.fori_loop(0, ROWS, turn, 0)

    def gathered(ref, i, plane, entries, cols):
        return jnp.concatenate(
            [jnp.concatenate([ref[tbl[plane + o, a, i]] for o in cols], axis=1) for a in entries], axis=0)

    def local_rows(start, count, plan):
        def step(n, carry):
            i = start + n
            lhs = jnp.concatenate([a_v[i, a] for a in range(5)], axis=1)
            for cols, keep, first_col in plan:
                got = jnp.dot(lhs, gathered(p_v, i, 0, range(5), cols), preferred_element_type=F32)
                lo = (cols[0] - first_col) * BLK
                hi = (cols[-1] + 1 - first_col) * BLK
                if keep is None:
                    m_v[i, :, lo:hi] = got.astype(BF16)
                else:
                    keep[n, :, lo:hi] = got
            return carry

        lax.fori_loop(0, count, step, 0)

    def lift(k, groups_of_cols):
        lhs = jnp.concatenate([pt[k * AGG + n] for n in range(AGG)], axis=1)
        for cols in groups_of_cols:
            rhs = m_v[k * AGG:(k + 1) * AGG, :, cols[0] * BLK:(cols[-1] + 1) * BLK]
            rhs = rhs.reshape(AGG * BLK, len(cols) * BLK)
            got = jnp.dot(lhs, rhs, preferred_element_type=F32)
            for t in range(3):
                for n, o in enumerate(cols):
                    co[k + t, o - t + 2] += got[t * BLK:(t + 1) * BLK, n * BLK:(n + 1) * BLK]

    a_copies[0].wait()
    local_rows(0, AGG, (((0, 1), acc_lo, 0), ((2,), acc_lo, 0), ((3, 4), None, 0)))
    lift(0, ((3, 4),))
    a_copies[1].wait()
    a_copies[2].wait()
    local_rows(AGG, 2 * AGG, (((0, 1), None, 0), ((2, 3), None, 0), ((4,), None, 0)))
    lift(1, ((0, 1), (2, 3), (4,)))
    lift(2, ((0, 1), (2, 3), (4,)))
    a_copies[3].wait()
    local_rows(3 * AGG, AGG, (((0, 1), None, 0), ((2, 3), acc_hi, 2), ((4,), acc_hi, 2)))
    lift(3, ((0, 1),))

    def pack(k, places):
        for place in places:
            s = (place + SHIFT[k]) % 7
            q, scale = quantised(co[k + 1, s])
            qb[k, place] = q
            sb[k, place:place + 1, :] = scale

    def owned(dest):
        k = AGGS
        for c in range(AGGS):
            k = jnp.where(owner[base + c] == dest, c, k)
        return k

    def to_owner(off, src, dst, send, recv, lo, hi):
        return pltpu.make_async_remote_copy(
            src_ref=src.at[off, pl.ds(lo, hi - lo)], dst_ref=dst.at[g, pl.ds(lo, hi - lo)],
            send_sem=send.at[off], recv_sem=recv.at[off],
            device_id=((g + off) % groups, r), device_id_type=MESH)

    def from_maker(off, src, dst, send, recv, lo, hi):
        return pltpu.make_async_remote_copy(
            src_ref=src.at[off, pl.ds(lo, hi - lo)],
            dst_ref=dst.at[(g + groups - off) % groups, pl.ds(lo, hi - lo)], send_sem=send.at[off],
            recv_sem=recv.at[off], device_id=((g + groups - off) % groups, r), device_id_type=MESH)

    order = (4, 3, 5, 2, 6, 1, 7)
    early = (sq, q_out, ge_send, ge_recv, 0, EARLY)
    late = (sq, q_out, gq_send, gq_recv, EARLY, 7)
    scales = (ss, sc_out, gs_send, gs_recv, 0, 8)
    vectors = (sx, xr_out, gx_send, gx_recv, 0, 8)
    qb[AGGS] = jnp.zeros_like(qb[AGGS])
    sb[...] = jnp.zeros_like(sb)
    for k in range(AGGS):
        pack(k, range(EARLY))
    for off in order + (0,):
        sq[off, 0:EARLY] = qb[owned((g + off) % groups), 0:EARLY]
        if off:
            to_owner(off, *early).start()

    def halo_rows(start, ref, keep, first_col):
        def step(n, carry):
            i = start + n
            lhs = jnp.concatenate([a_v[i, a] for a in range(1, 5)], axis=1)
            for cols in ((0, 1), (2,)):
                got = jnp.dot(lhs, gathered(ref, i, 5, range(1, 5), cols), preferred_element_type=F32)
                lo = cols[0] * BLK
                hi = (cols[-1] + 1) * BLK
                m_v[i, :, first_col * BLK + lo:first_col * BLK + hi] = (keep[n, :, lo:hi] + got).astype(BF16)
            return carry

        lax.fori_loop(0, AGG, step, 0)

    def send_partial(part, side, row, all_s, target, slot):
        lo, hi = ((0, 2), (2, 5))[part]
        ps_s[side, part] = jnp.zeros_like(ps_s[side, part])
        for n in range(lo, hi):
            q, scale = quantised(co[row, all_s[n]])
            pq_s[side, n] = q
            ps_s[side, part, n:n + 1, :] = scale
        copies = (
            to_neighbour(slot, pq_s.at[side, pl.ds(lo, hi - lo)], pq_r.at[side, pl.ds(lo, hi - lo)], target),
            to_neighbour(slot + 1, ps_s.at[side, part], ps_r.at[side, part], target),
        )
        for copy in copies:
            copy.start()
        return copies

    down = (5, 6, 2, 3, 4)
    up = (0, 1, 2, 3, 4)
    p_next.wait_recv()
    sent_down = send_partial(0, 0, 0, down, prv, 4)
    halo_rows(0, h_lo, acc_lo, 0)
    lift(0, ((0, 1), (2,)))
    sent_down += send_partial(1, 0, 0, down, prv, 6)
    p_prev.wait_recv()
    sent_up = send_partial(0, 1, 5, up, nxt, 8)
    halo_rows(3 * AGG, h_hi, acc_hi, 2)
    lift(3, ((2, 3), (4,)))
    sent_up += send_partial(1, 1, 5, up, nxt, 10)
    pack(1, range(EARLY, 7))
    pack(2, range(EARLY, 7))

    def receive_partial(copies, side, row, all_s):
        for copy in copies:
            copy.wait_recv()
        for n in range(5):
            part = 0 if n < 2 else 1
            co[row, all_s[n]] += pq_r[side, n].astype(jnp.int32).astype(F32) * ps_r[side, part, n:n + 1, :]

    receive_partial(sent_down, 0, AGGS, down)
    pack(3, range(EARLY, 7))
    receive_partial(sent_up, 1, 1, up)
    pack(0, range(EARLY, 7))
    for off in order + (0,):
        k = owned((g + off) % groups)
        sq[off, EARLY:7] = qb[k, EARLY:7]
        ss[off] = sb[k]
        if off:
            to_owner(off, *late).start()
            to_owner(off, *scales).start()
    own_q = pltpu.make_async_copy(sq.at[0], q_out.at[g], self_sem.at[0])
    own_s = pltpu.make_async_copy(ss.at[0], sc_out.at[g], self_sem.at[1])
    own_q.start()
    own_s.start()

    x_next.wait_recv()
    x_prev.wait_recv()
    center, old_weight, resid_weight = chebyshev_terms(
        jnp.full((1, BLK), lam_low[0], F32), jnp.full((1, BLK), lam_high[0], F32))

    def applied(k, mine, halo, scale_by):
        total = None
        for s in range(7):
            c = k + s - 3
            if c < 0:
                row = halo[0, AGGS + c:AGGS + c + 1, :]
            elif c < AGGS:
                row = mine[c:c + 1, :]
            else:
                row = halo[1, c - AGGS:c - AGGS + 1, :]
            if scale_by is not None:
                row = row / scale_by
            term = co[k + 1, s] * row
            total = term if total is None else total + term
        return jnp.sum(total.T, axis=0, keepdims=True)

    own2[...] = jnp.zeros_like(own2)
    for k in range(AGGS):
        rhs = own[k:k + 1, :]
        x1 = rhs / center
        own2[k:k + 1, :] = x1 + old_weight * x1 + resid_weight * (rhs - applied(k, own, halo_x, center))
    x2_next = to_neighbour(12, own2, halo_x2.at[0], nxt)
    x2_prev = to_neighbour(13, own2, halo_x2.at[1], prv)
    x2_next.start()
    x2_prev.start()
    xrb[...] = jnp.zeros_like(xrb)
    x2_next.wait_recv()
    x2_prev.wait_recv()
    for k in range(AGGS):
        xrb[k, 0:1, :] = own2[k:k + 1, :]
        xrb[k, 1:2, :] = own[k:k + 1, :] - applied(k, own2, halo_x2, None)
    for off in order + (0,):
        sx[off] = xrb[owned((g + off) % groups)]
        if off:
            to_owner(off, *vectors).start()
    own_x = pltpu.make_async_copy(sx.at[0], xr_out.at[g], self_sem.at[2])
    own_x.start()

    for copy in (p_next, p_prev, x_next, x_prev, *sent_down, *sent_up, x2_next, x2_prev):
        copy.wait_send()
    for off in order:
        for args in (early, late, scales, vectors):
            to_owner(off, *args).wait_send()
            from_maker(off, *args).wait_recv()
    own_q.wait()
    own_s.wait()
    own_x.wait()


def call_kernel(groups, rows_axis, pc, owner, lam_low, lam_high, fc, a, p, rhs):
    hbm = pl.BlockSpec(memory_space=pl.ANY)
    smem = pl.BlockSpec(memory_space=pltpu.SMEM)
    vmem = pl.BlockSpec(memory_space=pltpu.VMEM)
    dma = pltpu.SemaphoreType.DMA
    i16 = jnp.int16
    return pl.pallas_call(
        functools.partial(kernel, groups, rows_axis),
        out_shape=(
            jax.ShapeDtypeStruct((groups, 7, BLK, BLK), i16),
            jax.ShapeDtypeStruct((groups, 8, BLK), F32),
            jax.ShapeDtypeStruct((groups, 8, BLK), F32),
        ),
        in_specs=[smem, smem, smem, smem, vmem, hbm, hbm, vmem],
        out_specs=(hbm, hbm, hbm),
        scratch_shapes=[
            pltpu.VMEM((11, 8, BLK), jnp.int32),
            pltpu.SMEM((11, 8, BLK), jnp.int32),
            pltpu.VMEM((ROWS, 5, BLK, BLK), BF16),
            pltpu.VMEM((2 * ROWS + 1, BLK, BLK), BF16),
            pltpu.VMEM((2 * AGG + 1, BLK, BLK), BF16),
            pltpu.VMEM((2 * AGG + 1, BLK, BLK), BF16),
            pltpu.VMEM((ROWS, 3 * BLK, BLK), BF16),
            pltpu.VMEM((ROWS, BLK, 5 * BLK), BF16),
            pltpu.VMEM((AGG, BLK, 3 * BLK), F32),
            pltpu.VMEM((AGG, BLK, 3 * BLK), F32),
            pltpu.VMEM((AGGS + 2, 7, BLK, BLK), F32),
            pltpu.VMEM((AGGS + 1, 7, BLK, BLK), i16),
            pltpu.VMEM((AGGS + 1, 8, BLK), F32),
            pltpu.VMEM((groups, 7, BLK, BLK), i16),
            pltpu.VMEM((groups, 8, BLK), F32),
            pltpu.VMEM((AGGS + 1, 8, BLK), F32),
            pltpu.VMEM((groups, 8, BLK), F32),
            pltpu.VMEM((2, 5, BLK, BLK), i16),
            pltpu.VMEM((2, 2, 8, BLK), F32),
            pltpu.VMEM((2, 5, BLK, BLK), i16),
            pltpu.VMEM((2, 2, 8, BLK), F32),
            pltpu.VMEM((8, BLK), F32),
            pltpu.VMEM((2, 8, BLK), F32),
            pltpu.VMEM((8, BLK), F32),
            pltpu.VMEM((2, 8, BLK), F32),
            dma((AGGS,)), dma, dma, dma((14,)), dma((14,)),
            dma((groups,)), dma((groups,)), dma((groups,)), dma((groups,)),
            dma((groups,)), dma((groups,)), dma((groups,)), dma((groups,)),
            dma((3,)),
        ],
        compiler_params=pltpu.CompilerParams(
            collective_id=0, has_side_effects=True, vmem_limit_bytes=56 << 20),
    )(pc, owner, lam_low, lam_high, fc, a, p, rhs)


def open_slots(rows_axis, owner, q_ref, scale_ref, xr_ref, out_ref, x_ref, r_ref):
    slot = pl.program_id(0)
    g = lax.axis_index("grp")
    maker = slot * rows_axis + lax.axis_index("row")
    shift = 0
    for k in range(AGGS):
        shift = jnp.where(owner[maker * AGGS + k] == g, SHIFT[k], shift)
    for s in range(7):
        place = s - shift
        place = jnp.where(place < 0, place + 7, place)
        out_ref[0, s] = q_ref[0, place].astype(jnp.int32).astype(F32) * scale_ref[0, pl.ds(place, 1), :]

    @pl.when(slot == 0)
    def _():
        for n in range(x_ref.shape[0]):
            x_ref[n:n + 1, :] = xr_ref[n, 0:1, :]
            r_ref[n:n + 1, :] = xr_ref[n, 1:2, :]


def call_open(groups, rows_axis, owner, q, scale, xr):
    whole = pl.BlockSpec((groups, BLK), lambda n, owner: (0, 0))
    return pl.pallas_call(
        functools.partial(open_slots, rows_axis),
        out_shape=(
            jax.ShapeDtypeStruct((groups, 7, BLK, BLK), F32),
            jax.ShapeDtypeStruct((groups, BLK), F32),
            jax.ShapeDtypeStruct((groups, BLK), F32),
        ),
        grid_spec=pltpu.PrefetchScalarGridSpec(
            num_scalar_prefetch=1,
            grid=(groups,),
            in_specs=[
                pl.BlockSpec((1, 7, BLK, BLK), lambda n, owner: (n, 0, 0, 0)),
                pl.BlockSpec((1, 8, BLK), lambda n, owner: (n, 0, 0)),
                pl.BlockSpec((groups, 8, BLK), lambda n, owner: (0, 0, 0)),
            ],
            out_specs=(
                pl.BlockSpec((1, 7, BLK, BLK), lambda n, owner: (n, 0, 0, 0)),
                whole,
                whole,
            ),
        ),
    )(owner, q, scale, xr)


def per_device(
    fine_cols, fine_blocks, prolong_cols, prolong_blocks, agg_owner, coarse_rhs, lam_low, lam_high
):
    groups = lax.axis_size("grp")
    rows_axis = lax.axis_size("row")
    q, scale, xr = call_kernel(
        groups, rows_axis, prolong_cols.T, agg_owner, lam_low, lam_high, fine_cols.T, fine_blocks,
        prolong_blocks.reshape(2 * ROWS, BLK, BLK), coarse_rhs)
    return call_open(groups, rows_axis, agg_owner, q, scale, xr)


def solution(mesh):
    return jax.shard_map(
        per_device,
        mesh=mesh,
        in_specs=(
            P(("grp", "row"), None),
            P(("grp", "row"), None, None, None),
            P(),
            P(("grp", "row"), None, None, None),
            P(),
            P(("grp", "row"), None),
            P(),
            P(),
        ),
        out_specs=(
            P(("grp", "row"), None, None, None),
            P(("grp", "row"), None),
            P(("grp", "row"), None),
        ),
        check_vma=False,
    )
```

```python
import functools

import jax
import jax.numpy as jnp
from jax import lax
from jax.experimental import pallas as pl
from jax.experimental.pallas import tpu as pltpu
from jax.sharding import PartitionSpec as P

MESH = pl.DeviceIdType.MESH
BLK = 128
AGG = 10
AGGS = 4
ROWS = AGG * AGGS
F32 = jnp.float32
BF16 = jnp.bfloat16
Q_MAX = 32767.0
TINY = 2.0**-110
TRAVEL = ((5, 6, 0, 1, 4, 2, 3), (3, 4, 5, 6, 0, 1, 2), (0, 1, 2, 3, 6, 5, 4), (0, 1, 6, 5, 2, 4, 3))
CUTS = ((0, 3), (3, 5), (5, 7))
DOWN = (5, 6, 2, 3, 4)
UP = (0, 1, 4, 2, 3)
PARTS = ((0, 2), (2, 3), (3, 5))


def quantised(block):
    top = jnp.maximum(jnp.max(jnp.abs(block), axis=0, keepdims=True), TINY)
    q = jnp.floor(block * (Q_MAX / top) + 0.5).astype(jnp.int32).astype(jnp.int16)
    return q, top * (1.0 / Q_MAX)


def chebyshev_terms(low, high):
    center = 0.5 * (high + low)
    radius = 0.5 * (high - low)
    sigma_ratio = center / radius
    first_rho = 1.0 / sigma_ratio
    second_rho = 1.0 / (2.0 * sigma_ratio - first_rho)
    return center, second_rho * first_rho, 2.0 * second_rho / radius


def wrapped(x, total):
    x = jnp.where(x > total // 2, x - total, x)
    return jnp.where(x < -(total // 2), x + total, x)


def write_tables(fine_total, coarse_total, first_row, base, fc, pc, skip, tbl):
    row = lax.broadcasted_iota(jnp.int32, (5, ROWS), 1)
    reach = wrapped(fc[...] - (first_row + row), fine_total)
    place = row + AGG + reach
    near = [jnp.zeros((5, ROWS), jnp.int32) for _ in range(2)]
    for p in range(ROWS + 2 * AGG):
        for q in range(2):
            near[q] = jnp.where(place == p, pc[(skip + p) // BLK, q, (skip + p) % BLK], near[q])
    agg = jnp.zeros((5, ROWS), jnp.int32)
    for k in range(1, AGGS):
        agg = agg + jnp.where(row >= k * AGG, 1, 0)
    offset = [wrapped(c - base - agg, coarse_total) + 2 for c in near]

    def pick(o, ok, first, second, none):
        got = jnp.where(ok & (offset[0] == o), first, none)
        return jnp.where(ok & (offset[1] == o), second, got)

    inside = (place >= AGG) & (place < ROWS + AGG)
    mine = 2 * (place - AGG)
    for o in range(5):
        tbl[o, 0:5, 0:ROWS] = pick(o, inside, mine, mine + 1, 2 * ROWS)
    below = (place >= 0) & (place < AGG)
    above = (place >= ROWS + AGG) & (place < ROWS + 2 * AGG)
    high = place - ROWS - AGG
    low_part = jnp.where(below & (offset[0] == 0), place, AGG)
    high_part = jnp.where(above & (offset[1] == 4), high, AGG)
    tbl[5, 0:5, 0:ROWS] = jnp.where(row < 2 * AGG, low_part, high_part)
    for n in range(2):
        from_low = pick(1 + n, below, place, place + AGG, 2 * AGG)
        from_high = pick(2 + n, above, high + AGG, high, 2 * AGG)
        tbl[6 + n, 0:5, 0:ROWS] = jnp.where(row < 2 * AGG, from_low, from_high)
    everywhere = row >= 0
    for t in range(3):
        tbl[8 + t, 0:5, 0:ROWS] = pick(t + 1, everywhere, 2 * row, 2 * row + 1, 2 * ROWS)


def kernel(
    groups, rows_axis,
    owner, lam_low, lam_high, pc_hbm, fc, a_hbm, p_hbm, p_pairs, rhs_ref,
    q_out, sc_out, xr_out,
    pc, tbl_v, tbl, a_v, p_v, lo_part, lo_all, hi_part, hi_all, pt, m_v, acc_lo, acc_hi, co, qb, sb, sq, ss, xrb, sx,
    pq_s, ps_s, pq_r, ps_r, own, halo_x, own2, halo_x2, tot,
    a_sem, p_sem, t_sem, nb_send, nb_recv, g0_send, g0_recv, g1_send, g1_recv, g2_send, g2_recv,
    gs_send, gs_recv, gx_send, gx_recv, self_sem,
):
    g = lax.axis_index("grp")
    r = lax.axis_index("row")
    device = g * rows_axis + r
    devices = groups * rows_axis
    base = device * AGGS
    last = (r + 1) // rows_axis
    nxt = ((g + last) % groups, (r + 1) % rows_axis)
    first = (rows_axis - r) // rows_axis
    prv = ((g + groups - first) % groups, (r + rows_axis - 1) % rows_axis)

    barrier = pltpu.get_barrier_semaphore()
    for target in (nxt, prv):
        pl.semaphore_signal(barrier, inc=1, device_id=target, device_id_type=MESH)
    for off in range(1, groups):
        pl.semaphore_signal(barrier, inc=1, device_id=((g + off) % groups, r), device_id_type=MESH)

    fine_total = ROWS * devices
    start = (device * ROWS + fine_total - AGG) % fine_total
    chunk = start // BLK
    pc_copies = [
        pltpu.make_async_copy(
            pc_hbm.at[:, pl.ds(pl.multiple_of(((chunk + n) % (fine_total // BLK)) * BLK, BLK), BLK)], pc.at[n], t_sem.at[n])
        for n in range(2)
    ]
    for copy in pc_copies:
        copy.start()
    p_copy = pltpu.make_async_copy(p_hbm, p_v.at[pl.ds(0, 2 * ROWS)], p_sem)
    p_copy.start()
    a_copies = [
        pltpu.make_async_copy(a_hbm.at[pl.ds(k * AGG, AGG)], a_v.at[pl.ds(k * AGG, AGG)], a_sem.at[k])
        for k in range(AGGS)
    ]
    for k in (0, 3, 1, 2):
        a_copies[k].start()

    own[...] = jnp.zeros_like(own)
    own[0:AGGS, :] = rhs_ref[...]
    tbl_v[...] = jnp.zeros_like(tbl_v)
    pl.semaphore_wait(barrier, groups + 1)

    def to_neighbour(slot, src, dst, target):
        return pltpu.make_async_remote_copy(
            src_ref=src, dst_ref=dst, send_sem=nb_send.at[slot], recv_sem=nb_recv.at[slot],
            device_id=target, device_id_type=MESH)

    last_rows = pl.ds(ROWS - AGG, AGG)
    first_rows = pl.ds(0, AGG)
    rest = pl.ds(AGG, AGG)
    p_next = (
        to_neighbour(0, p_pairs.at[last_rows, 0], lo_part.at[first_rows], nxt),
        to_neighbour(1, p_pairs.at[last_rows, 1], lo_all.at[rest], nxt),
    )
    p_prev = (
        to_neighbour(2, p_pairs.at[first_rows, 1], hi_part.at[first_rows], prv),
        to_neighbour(3, p_pairs.at[first_rows, 0], hi_all.at[rest], prv),
    )
    for n in range(2):
        p_next[n].start()
        p_prev[n].start()
    x_next = to_neighbour(4, own, halo_x.at[0], nxt)
    x_prev = to_neighbour(5, own, halo_x.at[1], prv)
    x_next.start()
    x_prev.start()

    for copy in pc_copies:
        copy.wait()
    write_tables(fine_total, AGGS * devices, device * ROWS, base, fc, pc, start % BLK, tbl_v)
    t_copy = pltpu.make_async_copy(tbl_v, tbl, t_sem.at[2])
    t_copy.start()
    zero_block = jnp.zeros((BLK, BLK), BF16)
    p_v[2 * ROWS] = zero_block
    lo_part[AGG] = zero_block
    hi_part[AGG] = zero_block
    lo_all[2 * AGG] = zero_block
    hi_all[2 * AGG] = zero_block
    co[...] = jnp.zeros_like(co)
    t_copy.wait()
    p_copy.wait()

    def turn(i, carry):
        for t in range(3):
            pt[i, t * BLK:(t + 1) * BLK, :] = p_v[tbl[8 + t, 0, i]].T
        return carry

    lax.fori_loop(0, ROWS, turn, 0)

    def gathered(ref, i, plane, entries, cols):
        return jnp.concatenate(
            [jnp.concatenate([ref[tbl[plane + o, a, i]] for o in cols], axis=1) for a in entries], axis=0)

    def local_rows(start, count, plan):
        def step(n, carry):
            i = start + n
            lhs = jnp.concatenate([a_v[i, a] for a in range(5)], axis=1)
            for cols, keep, first_col in plan:
                got = jnp.dot(lhs, gathered(p_v, i, 0, range(5), cols), preferred_element_type=F32)
                lo = (cols[0] - first_col) * BLK
                hi = (cols[-1] + 1 - first_col) * BLK
                if keep is None:
                    m_v[i, :, lo:hi] = got.astype(BF16)
                else:
                    keep[n, :, lo:hi] = got
            return carry

        lax.fori_loop(0, count, step, 0)

    def lift(k, groups_of_cols):
        lhs = jnp.concatenate([pt[k * AGG + n] for n in range(AGG)], axis=1)
        for cols in groups_of_cols:
            rhs = m_v[k * AGG:(k + 1) * AGG, :, cols[0] * BLK:(cols[-1] + 1) * BLK]
            rhs = rhs.reshape(AGG * BLK, len(cols) * BLK)
            got = jnp.dot(lhs, rhs, preferred_element_type=F32)
            for t in range(3):
                for n, o in enumerate(cols):
                    co[k + t, o - t + 2] += got[t * BLK:(t + 1) * BLK, n * BLK:(n + 1) * BLK]

    def send_partial(part, side):
        row, all_s, target = ((0, DOWN, prv), (AGGS + 1, UP, nxt))[side]
        lo, hi = PARTS[part]
        ps_s[side, part] = jnp.zeros_like(ps_s[side, part])
        for n in range(lo, hi):
            q, scale = quantised(co[row, all_s[n]])
            pq_s[side, n] = q
            ps_s[side, part, n:n + 1, :] = scale
        slot = 6 + 4 * part + 2 * side
        copies = (
            to_neighbour(slot, pq_s.at[side, pl.ds(lo, hi - lo)], pq_r.at[side, pl.ds(lo, hi - lo)], target),
            to_neighbour(slot + 1, ps_s.at[side, part], ps_r.at[side, part], target),
        )
        for copy in copies:
            copy.start()
        return copies

    def receive_partial(copies, part, side):
        row, all_s = ((AGGS, DOWN), (1, UP))[side]
        for copy in copies:
            copy.wait_recv()
        for n in range(*PARTS[part]):
            co[row, all_s[n]] += pq_r[side, n].astype(jnp.int32).astype(F32) * ps_r[side, part, n:n + 1, :]

    a_copies[0].wait()
    local_rows(0, AGG, (((0, 1), acc_lo, 0), ((2,), acc_lo, 0), ((3, 4), None, 0)))
    lift(0, ((3, 4),))
    sent = {(0, 0): send_partial(0, 0)}
    a_copies[3].wait()
    local_rows(3 * AGG, AGG, (((0, 1), None, 0), ((2, 3), acc_hi, 2), ((4,), acc_hi, 2)))
    lift(3, ((0, 1),))
    sent[0, 1] = send_partial(0, 1)
    a_copies[1].wait()
    a_copies[2].wait()
    local_rows(AGG, 2 * AGG, (((0, 1), None, 0), ((2, 3), None, 0), ((4,), None, 0)))
    lift(1, ((0, 1), (2, 3), (4,)))
    lift(2, ((0, 1), (2, 3), (4,)))

    def pack(k, places):
        for place in places:
            q, scale = quantised(co[k + 1, TRAVEL[k][place]])
            qb[k, place] = q
            sb[k, place:place + 1, :] = scale

    def owned(dest):
        k = AGGS
        for c in range(AGGS):
            k = jnp.where(owner[base + c] == dest, c, k)
        return k

    def to_owner(off, src, dst, send, recv, lo, hi):
        return pltpu.make_async_remote_copy(
            src_ref=src.at[off, pl.ds(lo, hi - lo)], dst_ref=dst.at[g, pl.ds(lo, hi - lo)],
            send_sem=send.at[off], recv_sem=recv.at[off],
            device_id=((g + off) % groups, r), device_id_type=MESH)

    def from_maker(off, src, dst, send, recv, lo, hi):
        return pltpu.make_async_remote_copy(
            src_ref=src.at[off, pl.ds(lo, hi - lo)],
            dst_ref=dst.at[(g + groups - off) % groups, pl.ds(lo, hi - lo)], send_sem=send.at[off],
            recv_sem=recv.at[off], device_id=((g + groups - off) % groups, r), device_id_type=MESH)

    order = (4, 3, 5, 2, 6, 1, 7)
    parts = (
        (sq, q_out, g0_send, g0_recv, *CUTS[0]),
        (sq, q_out, g1_send, g1_recv, *CUTS[1]),
        (sq, q_out, g2_send, g2_recv, *CUTS[2]),
    )
    scales = (ss, sc_out, gs_send, gs_recv, 0, 8)
    vectors = (sx, xr_out, gx_send, gx_recv, 0, 8)

    def repartition(part):
        lo, hi = CUTS[part]
        for off in order + (0,):
            sq[off, lo:hi] = qb[owned((g + off) % groups), lo:hi]
            if off:
                to_owner(off, *parts[part]).start()

    qb[AGGS] = jnp.zeros_like(qb[AGGS])
    sb[...] = jnp.zeros_like(sb)
    for side in range(2):
        receive_partial(sent[0, side], 0, side)
    for k in range(AGGS):
        pack(k, range(*CUTS[0]))
    repartition(0)

    def halo_rows(start, ref, plane, count, keep, keep_col, first_col):
        width = count * BLK

        def step(n, carry):
            i = start + n
            lhs = jnp.concatenate([a_v[i, a] for a in range(1, 5)], axis=1)
            got = jnp.dot(lhs, gathered(ref, i, plane, range(1, 5), range(count)), preferred_element_type=F32)
            got = got + keep[n, :, keep_col * BLK:keep_col * BLK + width]
            m_v[i, :, first_col * BLK:first_col * BLK + width] = got.astype(BF16)
            return carry

        lax.fori_loop(0, AGG, step, 0)

    p_next[0].wait_recv()
    halo_rows(0, lo_part, 5, 1, acc_lo, 0, 0)
    lift(0, ((0,),))
    sent[1, 0] = send_partial(1, 0)
    p_prev[0].wait_recv()
    halo_rows(3 * AGG, hi_part, 5, 1, acc_hi, 2, 4)
    lift(3, ((4,),))
    sent[1, 1] = send_partial(1, 1)
    lo_all[0:AGG] = lo_part[0:AGG]
    hi_all[0:AGG] = hi_part[0:AGG]
    p_next[1].wait_recv()
    halo_rows(0, lo_all, 6, 2, acc_lo, 1, 1)
    lift(0, ((1, 2),))
    sent[2, 0] = send_partial(2, 0)
    p_prev[1].wait_recv()
    halo_rows(3 * AGG, hi_all, 6, 2, acc_hi, 0, 2)
    lift(3, ((2, 3),))
    sent[2, 1] = send_partial(2, 1)

    for side in range(2):
        receive_partial(sent[1, side], 1, side)
    for k in range(AGGS):
        pack(k, range(*CUTS[1]))
    repartition(1)
    pack(1, range(*CUTS[2]))
    pack(2, range(*CUTS[2]))

    x_next.wait_recv()
    x_prev.wait_recv()
    center, old_weight, resid_weight = chebyshev_terms(
        jnp.full((1, BLK), lam_low[0], F32), jnp.full((1, BLK), lam_high[0], F32))

    def products(k, mine, halo, scale_by, of_mine, of_halo):
        total = jnp.zeros((BLK, BLK), F32)
        for s in range(7):
            c = k + s - 3
            here = 0 <= c < AGGS
            if not (of_mine if here else of_halo):
                continue
            if here:
                row = mine[c:c + 1, :]
            elif c < 0:
                row = halo[0, AGGS + c:AGGS + c + 1, :]
            else:
                row = halo[1, c - AGGS:c - AGGS + 1, :]
            if scale_by is not None:
                row = row / scale_by
            total = total + co[k + 1, s] * row
        return total

    def summed(total):
        return jnp.sum(total.T, axis=0, keepdims=True)

    own2[...] = jnp.zeros_like(own2)
    xrb[...] = jnp.zeros_like(xrb)

    def first_sweep(k):
        rhs = own[k:k + 1, :]
        x1 = rhs / center
        residual = rhs - summed(products(k, own, halo_x, center, True, True))
        x2 = x1 + old_weight * x1 + resid_weight * residual
        own2[k:k + 1, :] = x2
        xrb[k, 0:1, :] = x2

    first_sweep(1)
    first_sweep(2)
    receive_partial(sent[2, 0], 2, 0)
    first_sweep(3)
    receive_partial(sent[2, 1], 2, 1)
    first_sweep(0)
    x2_next = to_neighbour(18, own2, halo_x2.at[0], nxt)
    x2_prev = to_neighbour(19, own2, halo_x2.at[1], prv)
    x2_next.start()
    x2_prev.start()
    pack(3, range(*CUTS[2]))
    pack(0, range(*CUTS[2]))
    repartition(2)
    for off in order + (0,):
        ss[off] = sb[owned((g + off) % groups)]
        if off:
            to_owner(off, *scales).start()
    own_q = pltpu.make_async_copy(sq.at[0], q_out.at[g], self_sem.at[0])
    own_s = pltpu.make_async_copy(ss.at[0], sc_out.at[g], self_sem.at[1])
    own_q.start()
    own_s.start()
    for k in range(AGGS):
        tot[k] = products(k, own2, halo_x2, None, True, False)
    x2_next.wait_recv()
    x2_prev.wait_recv()
    for k in range(AGGS):
        total = tot[k] + products(k, own2, halo_x2, None, False, True)
        xrb[k, 1:2, :] = own[k:k + 1, :] - summed(total)
    for off in order + (0,):
        sx[off] = xrb[owned((g + off) % groups)]
        if off:
            to_owner(off, *vectors).start()
    own_x = pltpu.make_async_copy(sx.at[0], xr_out.at[g], self_sem.at[2])
    own_x.start()

    for copy in (*p_next, *p_prev, x_next, x_prev, x2_next, x2_prev):
        copy.wait_send()
    for copies in sent.values():
        for copy in copies:
            copy.wait_send()
    for off in order:
        for args in (*parts, scales, vectors):
            to_owner(off, *args).wait_send()
            from_maker(off, *args).wait_recv()
    own_q.wait()
    own_s.wait()
    own_x.wait()


def call_kernel(groups, rows_axis, owner, lam_low, lam_high, pc, fc, a, p, rhs):
    hbm = pl.BlockSpec(memory_space=pl.ANY)
    smem = pl.BlockSpec(memory_space=pltpu.SMEM)
    vmem = pl.BlockSpec(memory_space=pltpu.VMEM)
    dma = pltpu.SemaphoreType.DMA
    i16 = jnp.int16
    return pl.pallas_call(
        functools.partial(kernel, groups, rows_axis),
        out_shape=(
            jax.ShapeDtypeStruct((groups, 7, BLK, BLK), i16),
            jax.ShapeDtypeStruct((groups, 8, BLK), F32),
            jax.ShapeDtypeStruct((groups, 8, BLK), F32),
        ),
        in_specs=[smem, smem, smem, hbm, vmem, hbm, hbm, hbm, vmem],
        out_specs=(hbm, hbm, hbm),
        scratch_shapes=[
            pltpu.SMEM((2, 2, BLK), jnp.int32),
            pltpu.VMEM((11, 8, BLK), jnp.int32),
            pltpu.SMEM((11, 8, BLK), jnp.int32),
            pltpu.VMEM((ROWS, 5, BLK, BLK), BF16),
            pltpu.VMEM((2 * ROWS + 1, BLK, BLK), BF16),
            pltpu.VMEM((AGG + 1, BLK, BLK), BF16),
            pltpu.VMEM((2 * AGG + 1, BLK, BLK), BF16),
            pltpu.VMEM((AGG + 1, BLK, BLK), BF16),
            pltpu.VMEM((2 * AGG + 1, BLK, BLK), BF16),
            pltpu.VMEM((ROWS, 3 * BLK, BLK), BF16),
            pltpu.VMEM((ROWS, BLK, 5 * BLK), BF16),
            pltpu.VMEM((AGG, BLK, 3 * BLK), F32),
            pltpu.VMEM((AGG, BLK, 3 * BLK), F32),
            pltpu.VMEM((AGGS + 2, 7, BLK, BLK), F32),
            pltpu.VMEM((AGGS + 1, 7, BLK, BLK), i16),
            pltpu.VMEM((AGGS + 1, 8, BLK), F32),
            pltpu.VMEM((groups, 7, BLK, BLK), i16),
            pltpu.VMEM((groups, 8, BLK), F32),
            pltpu.VMEM((AGGS + 1, 8, BLK), F32),
            pltpu.VMEM((groups, 8, BLK), F32),
            pltpu.VMEM((2, 5, BLK, BLK), i16),
            pltpu.VMEM((2, 3, 8, BLK), F32),
            pltpu.VMEM((2, 5, BLK, BLK), i16),
            pltpu.VMEM((2, 3, 8, BLK), F32),
            pltpu.VMEM((8, BLK), F32),
            pltpu.VMEM((2, 8, BLK), F32),
            pltpu.VMEM((8, BLK), F32),
            pltpu.VMEM((2, 8, BLK), F32),
            pltpu.VMEM((AGGS, BLK, BLK), F32),
            dma((AGGS,)), dma, dma((3,)), dma((20,)), dma((20,)),
            dma((groups,)), dma((groups,)),
            dma((groups,)), dma((groups,)), dma((groups,)), dma((groups,)),
            dma((groups,)), dma((groups,)), dma((groups,)), dma((groups,)),
            dma((3,)),
        ],
        compiler_params=pltpu.CompilerParams(
            collective_id=0, has_side_effects=True, vmem_limit_bytes=56 << 20),
    )(owner, lam_low, lam_high, pc, fc, a, p.reshape(2 * ROWS, BLK, BLK), p, rhs)


def open_slots(groups, rows_axis, owner, q_hbm, scale, xr, out_hbm, x_ref, r_ref, q_v, o_v, in_sem, out_sem):
    g = lax.axis_index("grp")
    r = lax.axis_index("row")

    def arrive(n):
        return pltpu.make_async_copy(q_hbm.at[n], q_v.at[n], in_sem.at[n])

    def leave(n):
        return pltpu.make_async_copy(o_v.at[n], out_hbm.at[n], out_sem.at[n])

    for n in range(groups):
        arrive(n).start()
    for n in range(groups):
        x_ref[n:n + 1, :] = xr[n, 0:1, :]
        r_ref[n:n + 1, :] = xr[n, 1:2, :]

    def step(n, carry):
        first = (n * rows_axis + r) * AGGS
        places = [TRAVEL[0].index(s) for s in range(7)]
        for k in range(1, AGGS):
            mine = owner[first + k] == g
            places = [jnp.where(mine, TRAVEL[k].index(s), places[s]) for s in range(7)]
        arrive(n).wait()
        for s in range(7):
            o_v[n, s] = q_v[n, places[s]].astype(jnp.int32).astype(F32) * scale[n, pl.ds(places[s], 1), :]
        leave(n).start()
        return carry

    lax.fori_loop(0, groups, step, 0)
    for n in range(groups):
        leave(n).wait()


def call_open(groups, rows_axis, owner, q, scale, xr):
    hbm = pl.BlockSpec(memory_space=pl.ANY)
    vmem = pl.BlockSpec(memory_space=pltpu.VMEM)
    return pl.pallas_call(
        functools.partial(open_slots, groups, rows_axis),
        out_shape=(
            jax.ShapeDtypeStruct((groups, 7, BLK, BLK), F32),
            jax.ShapeDtypeStruct((groups, BLK), F32),
            jax.ShapeDtypeStruct((groups, BLK), F32),
        ),
        in_specs=[pl.BlockSpec(memory_space=pltpu.SMEM), hbm, vmem, vmem],
        out_specs=(hbm, vmem, vmem),
        scratch_shapes=[
            pltpu.VMEM((groups, 7, BLK, BLK), jnp.int16),
            pltpu.VMEM((groups, 7, BLK, BLK), F32),
            pltpu.SemaphoreType.DMA((groups,)),
            pltpu.SemaphoreType.DMA((groups,)),
        ],
    )(owner, q, scale, xr)


def per_device(
    fine_cols, fine_blocks, prolong_cols, prolong_blocks, agg_owner, coarse_rhs, lam_low, lam_high
):
    groups = lax.axis_size("grp")
    rows_axis = lax.axis_size("row")
    q, scale, xr = call_kernel(
        groups, rows_axis, agg_owner, lam_low, lam_high, prolong_cols.T, fine_cols.T, fine_blocks, prolong_blocks,
        coarse_rhs)
    return call_open(groups, rows_axis, agg_owner, q, scale, xr)


def solution(mesh):
    return jax.shard_map(
        per_device,
        mesh=mesh,
        in_specs=(
            P(("grp", "row"), None),
            P(("grp", "row"), None, None, None),
            P(),
            P(("grp", "row"), None, None, None),
            P(),
            P(("grp", "row"), None),
            P(),
            P(),
        ),
        out_specs=(
            P(("grp", "row"), None, None, None),
            P(("grp", "row"), None),
            P(("grp", "row"), None),
        ),
        check_vma=False,
    )
```

```python
import functools

import jax
import jax.numpy as jnp
from jax import lax
from jax.experimental import pallas as pl
from jax.experimental.pallas import tpu as pltpu
from jax.sharding import PartitionSpec as P

MESH = pl.DeviceIdType.MESH
BLK = 128
AGG = 10
AGGS = 4
ROWS = AGG * AGGS
F32 = jnp.float32
BF16 = jnp.bfloat16
Q_MAX = 32767.0
TINY = 2.0**-110
TOGETHER = 5
TRAVEL = ((5, 6, 0, 1, 4, 2, 3), (3, 4, 5, 6, 0, 1, 2), (0, 1, 2, 3, 6, 5, 4), (0, 1, 6, 5, 2, 4, 3))
CUTS = ((0, 3), (3, 5), (5, 7))
DOWN = (5, 6, 2, 3, 4)
UP = (0, 1, 4, 2, 3)
PARTS = ((0, 2), (2, 3), (3, 5))


def quantised(block):
    top = jnp.maximum(jnp.max(jnp.abs(block), axis=0, keepdims=True), TINY)
    q = jnp.floor(block * (Q_MAX / top) + 0.5).astype(jnp.int32).astype(jnp.int16)
    return q, top * (1.0 / Q_MAX)


def chebyshev_terms(low, high):
    center = 0.5 * (high + low)
    radius = 0.5 * (high - low)
    sigma_ratio = center / radius
    first_rho = 1.0 / sigma_ratio
    second_rho = 1.0 / (2.0 * sigma_ratio - first_rho)
    return center, second_rho * first_rho, 2.0 * second_rho / radius


def wrapped(x, total):
    x = jnp.where(x > total // 2, x - total, x)
    return jnp.where(x < -(total // 2), x + total, x)


def write_tables(fine_total, coarse_total, first_row, base, fc, pc, skip, tbl):
    row = lax.broadcasted_iota(jnp.int32, (5, ROWS), 1)
    reach = wrapped(fc[...] - (first_row + row), fine_total)
    place = row + AGG + reach
    near = [jnp.zeros((5, ROWS), jnp.int32) for _ in range(2)]
    for p in range(ROWS + 2 * AGG):
        for q in range(2):
            near[q] = jnp.where(place == p, pc[(skip + p) // BLK, q, (skip + p) % BLK], near[q])
    agg = jnp.zeros((5, ROWS), jnp.int32)
    for k in range(1, AGGS):
        agg = agg + jnp.where(row >= k * AGG, 1, 0)
    offset = [wrapped(c - base - agg, coarse_total) + 2 for c in near]

    def pick(o, ok, first, second, none):
        got = jnp.where(ok & (offset[0] == o), first, none)
        return jnp.where(ok & (offset[1] == o), second, got)

    inside = (place >= AGG) & (place < ROWS + AGG)
    mine = 2 * (place - AGG)
    for o in range(5):
        tbl[o, 0:5, 0:ROWS] = pick(o, inside, mine, mine + 1, 2 * ROWS)
    below = (place >= 0) & (place < AGG)
    above = (place >= ROWS + AGG) & (place < ROWS + 2 * AGG)
    high = place - ROWS - AGG
    low_part = jnp.where(below & (offset[0] == 0), place, AGG)
    high_part = jnp.where(above & (offset[1] == 4), high, AGG)
    tbl[5, 0:5, 0:ROWS] = jnp.where(row < 2 * AGG, low_part, high_part)
    for n in range(2):
        from_low = pick(1 + n, below, place, place + AGG, 2 * AGG)
        from_high = pick(2 + n, above, high + AGG, high, 2 * AGG)
        tbl[6 + n, 0:5, 0:ROWS] = jnp.where(row < 2 * AGG, from_low, from_high)
    everywhere = row >= 0
    for t in range(3):
        tbl[8 + t, 0:5, 0:ROWS] = pick(t + 1, everywhere, 2 * row, 2 * row + 1, 2 * ROWS)


def kernel(
    groups, rows_axis,
    owner, lam_low, lam_high, pc_hbm, fc, a_hbm, p_hbm, p_pairs, rhs_ref,
    q_out, sc_out, xr_out,
    pc, tbl_v, tbl, a_v, p_v, lo_part, lo_all, hi_part, hi_all, pt, m_v, acc_lo, acc_hi, co, qb, sb, sq, ss, xrb, sx,
    pq_s, ps_s, pq_r, ps_r, own, halo_x, own2, halo_x2, tot,
    a_sem, p_sem, t_sem, nb_send, nb_recv, g0_send, g0_recv, g1_send, g1_recv, g2_send, g2_recv,
    gs_send, gs_recv, gx_send, gx_recv, self_sem,
):
    g = lax.axis_index("grp")
    r = lax.axis_index("row")
    device = g * rows_axis + r
    devices = groups * rows_axis
    base = device * AGGS
    last = (r + 1) // rows_axis
    nxt = ((g + last) % groups, (r + 1) % rows_axis)
    first = (rows_axis - r) // rows_axis
    prv = ((g + groups - first) % groups, (r + rows_axis - 1) % rows_axis)

    barrier = pltpu.get_barrier_semaphore()
    for target in (nxt, prv):
        pl.semaphore_signal(barrier, inc=1, device_id=target, device_id_type=MESH)
    for off in range(1, groups):
        pl.semaphore_signal(barrier, inc=1, device_id=((g + off) % groups, r), device_id_type=MESH)

    fine_total = ROWS * devices
    start = (device * ROWS + fine_total - AGG) % fine_total
    chunk = start // BLK
    pc_copies = [
        pltpu.make_async_copy(
            pc_hbm.at[:, pl.ds(pl.multiple_of(((chunk + n) % (fine_total // BLK)) * BLK, BLK), BLK)], pc.at[n], t_sem.at[n])
        for n in range(2)
    ]
    for copy in pc_copies:
        copy.start()
    p_copy = pltpu.make_async_copy(p_hbm, p_v.at[pl.ds(0, 2 * ROWS)], p_sem)
    p_copy.start()
    a_copies = [
        pltpu.make_async_copy(a_hbm.at[pl.ds(k * AGG, AGG)], a_v.at[pl.ds(k * AGG, AGG)], a_sem.at[k])
        for k in range(AGGS)
    ]
    for k in (0, 3, 1, 2):
        a_copies[k].start()

    own[...] = jnp.zeros_like(own)
    own[0:AGGS, :] = rhs_ref[...]
    tbl_v[...] = jnp.zeros_like(tbl_v)
    pl.semaphore_wait(barrier, groups + 1)

    def to_neighbour(slot, src, dst, target):
        return pltpu.make_async_remote_copy(
            src_ref=src, dst_ref=dst, send_sem=nb_send.at[slot], recv_sem=nb_recv.at[slot],
            device_id=target, device_id_type=MESH)

    last_rows = pl.ds(ROWS - AGG, AGG)
    first_rows = pl.ds(0, AGG)
    rest = pl.ds(AGG, AGG)
    p_next = (
        to_neighbour(0, p_pairs.at[last_rows, 0], lo_part.at[first_rows], nxt),
        to_neighbour(1, p_pairs.at[last_rows, 1], lo_all.at[rest], nxt),
    )
    p_prev = (
        to_neighbour(2, p_pairs.at[first_rows, 1], hi_part.at[first_rows], prv),
        to_neighbour(3, p_pairs.at[first_rows, 0], hi_all.at[rest], prv),
    )
    p_next[0].start()
    p_prev[0].start()
    x_next = to_neighbour(4, own, halo_x.at[0], nxt)
    x_prev = to_neighbour(5, own, halo_x.at[1], prv)
    x_next.start()
    x_prev.start()

    for copy in pc_copies:
        copy.wait()
    write_tables(fine_total, AGGS * devices, device * ROWS, base, fc, pc, start % BLK, tbl_v)
    t_copy = pltpu.make_async_copy(tbl_v, tbl, t_sem.at[2])
    t_copy.start()
    zero_block = jnp.zeros((BLK, BLK), BF16)
    p_v[2 * ROWS] = zero_block
    lo_part[AGG] = zero_block
    hi_part[AGG] = zero_block
    lo_all[2 * AGG] = zero_block
    hi_all[2 * AGG] = zero_block
    co[...] = jnp.zeros_like(co)
    t_copy.wait()
    p_copy.wait()

    def for_rows(count, body):
        def step(n, carry):
            for m in range(TOGETHER):
                body(n * TOGETHER + m)
            return carry

        lax.fori_loop(0, count // TOGETHER, step, 0)

    def turn(i):
        for t in range(3):
            pt[i, t * BLK:(t + 1) * BLK, :] = p_v[tbl[8 + t, 0, i]].T

    for_rows(ROWS, turn)

    def gathered(ref, i, plane, entries, cols):
        return jnp.concatenate(
            [jnp.concatenate([ref[tbl[plane + o, a, i]] for o in cols], axis=1) for a in entries], axis=0)

    def local_rows(start, count, plan):
        def body(n):
            i = start + n
            lhs = jnp.concatenate([a_v[i, a] for a in range(5)], axis=1)
            for cols, keep, first_col in plan:
                got = jnp.dot(lhs, gathered(p_v, i, 0, range(5), cols), preferred_element_type=F32)
                lo = (cols[0] - first_col) * BLK
                hi = (cols[-1] + 1 - first_col) * BLK
                if keep is None:
                    m_v[i, :, lo:hi] = got.astype(BF16)
                else:
                    keep[n, :, lo:hi] = got

        for_rows(count, body)

    def lift(k, groups_of_cols):
        lhs = jnp.concatenate([pt[k * AGG + n] for n in range(AGG)], axis=1)
        for cols in groups_of_cols:
            rhs = m_v[k * AGG:(k + 1) * AGG, :, cols[0] * BLK:(cols[-1] + 1) * BLK]
            rhs = rhs.reshape(AGG * BLK, len(cols) * BLK)
            got = jnp.dot(lhs, rhs, preferred_element_type=F32)
            for t in range(3):
                for n, o in enumerate(cols):
                    co[k + t, o - t + 2] += got[t * BLK:(t + 1) * BLK, n * BLK:(n + 1) * BLK]

    def send_partial(part, side):
        row, all_s, target = ((0, DOWN, prv), (AGGS + 1, UP, nxt))[side]
        lo, hi = PARTS[part]
        ps_s[side, part] = jnp.zeros_like(ps_s[side, part])
        for n in range(lo, hi):
            q, scale = quantised(co[row, all_s[n]])
            pq_s[side, n] = q
            ps_s[side, part, n:n + 1, :] = scale
        slot = 6 + 4 * part + 2 * side
        copies = (
            to_neighbour(slot, pq_s.at[side, pl.ds(lo, hi - lo)], pq_r.at[side, pl.ds(lo, hi - lo)], target),
            to_neighbour(slot + 1, ps_s.at[side, part], ps_r.at[side, part], target),
        )
        for copy in copies:
            copy.start()
        return copies

    def receive_partial(copies, part, side):
        row, all_s = ((AGGS, DOWN), (1, UP))[side]
        for copy in copies:
            copy.wait_recv()
        for n in range(*PARTS[part]):
            co[row, all_s[n]] += pq_r[side, n].astype(jnp.int32).astype(F32) * ps_r[side, part, n:n + 1, :]

    a_copies[0].wait()
    local_rows(0, AGG, (((0, 1), acc_lo, 0), ((2,), acc_lo, 0), ((3, 4), None, 0)))
    lift(0, ((3, 4),))
    sent = {(0, 0): send_partial(0, 0)}
    a_copies[3].wait()
    local_rows(3 * AGG, AGG, (((0, 1), None, 0), ((2, 3), acc_hi, 2), ((4,), acc_hi, 2)))
    lift(3, ((0, 1),))
    sent[0, 1] = send_partial(0, 1)
    p_next[0].wait_send()
    p_next[1].start()
    p_prev[0].wait_send()
    p_prev[1].start()
    a_copies[1].wait()
    a_copies[2].wait()
    local_rows(AGG, 2 * AGG, (((0, 1), None, 0), ((2, 3), None, 0), ((4,), None, 0)))
    lift(1, ((0, 1), (2, 3), (4,)))
    lift(2, ((0, 1), (2, 3), (4,)))

    def pack(k, places):
        for place in places:
            q, scale = quantised(co[k + 1, TRAVEL[k][place]])
            qb[k, place] = q
            sb[k, place:place + 1, :] = scale

    def owned(dest):
        k = AGGS
        for c in range(AGGS):
            k = jnp.where(owner[base + c] == dest, c, k)
        return k

    def to_owner(off, src, dst, send, recv, lo, hi):
        return pltpu.make_async_remote_copy(
            src_ref=src.at[off, pl.ds(lo, hi - lo)], dst_ref=dst.at[g, pl.ds(lo, hi - lo)],
            send_sem=send.at[off], recv_sem=recv.at[off],
            device_id=((g + off) % groups, r), device_id_type=MESH)

    def from_maker(off, src, dst, send, recv, lo, hi):
        return pltpu.make_async_remote_copy(
            src_ref=src.at[off, pl.ds(lo, hi - lo)],
            dst_ref=dst.at[(g + groups - off) % groups, pl.ds(lo, hi - lo)], send_sem=send.at[off],
            recv_sem=recv.at[off], device_id=((g + groups - off) % groups, r), device_id_type=MESH)

    order = (4, 3, 5, 2, 6, 1, 7)
    parts = (
        (sq, q_out, g0_send, g0_recv, *CUTS[0]),
        (sq, q_out, g1_send, g1_recv, *CUTS[1]),
        (sq, q_out, g2_send, g2_recv, *CUTS[2]),
    )
    scales = (ss, sc_out, gs_send, gs_recv, 0, 8)
    vectors = (sx, xr_out, gx_send, gx_recv, 0, 8)

    def repartition(part):
        lo, hi = CUTS[part]
        for off in order + (0,):
            sq[off, lo:hi] = qb[owned((g + off) % groups), lo:hi]
            if off:
                to_owner(off, *parts[part]).start()

    qb[AGGS] = jnp.zeros_like(qb[AGGS])
    sb[...] = jnp.zeros_like(sb)
    for side in range(2):
        receive_partial(sent[0, side], 0, side)
    for k in range(AGGS):
        pack(k, range(*CUTS[0]))
    repartition(0)

    def halo_rows(start, ref, plane, count, keep, keep_col, first_col):
        width = count * BLK

        def body(n):
            i = start + n
            lhs = jnp.concatenate([a_v[i, a] for a in range(1, 5)], axis=1)
            got = jnp.dot(lhs, gathered(ref, i, plane, range(1, 5), range(count)), preferred_element_type=F32)
            got = got + keep[n, :, keep_col * BLK:keep_col * BLK + width]
            m_v[i, :, first_col * BLK:first_col * BLK + width] = got.astype(BF16)

        for_rows(AGG, body)

    p_next[0].wait_recv()
    halo_rows(0, lo_part, 5, 1, acc_lo, 0, 0)
    lift(0, ((0,),))
    sent[1, 0] = send_partial(1, 0)
    p_prev[0].wait_recv()
    halo_rows(3 * AGG, hi_part, 5, 1, acc_hi, 2, 4)
    lift(3, ((4,),))
    sent[1, 1] = send_partial(1, 1)
    lo_all[0:AGG] = lo_part[0:AGG]
    hi_all[0:AGG] = hi_part[0:AGG]
    p_next[1].wait_recv()
    halo_rows(0, lo_all, 6, 2, acc_lo, 1, 1)
    lift(0, ((1, 2),))
    sent[2, 0] = send_partial(2, 0)
    p_prev[1].wait_recv()
    halo_rows(3 * AGG, hi_all, 6, 2, acc_hi, 0, 2)
    lift(3, ((2, 3),))
    sent[2, 1] = send_partial(2, 1)

    for side in range(2):
        receive_partial(sent[1, side], 1, side)
    for k in range(AGGS):
        pack(k, range(*CUTS[1]))
    repartition(1)
    pack(1, range(*CUTS[2]))
    pack(2, range(*CUTS[2]))

    x_next.wait_recv()
    x_prev.wait_recv()
    center, old_weight, resid_weight = chebyshev_terms(
        jnp.full((1, BLK), lam_low[0], F32), jnp.full((1, BLK), lam_high[0], F32))

    def products(k, mine, halo, scale_by, of_mine, of_halo):
        total = jnp.zeros((BLK, BLK), F32)
        for s in range(7):
            c = k + s - 3
            here = 0 <= c < AGGS
            if not (of_mine if here else of_halo):
                continue
            if here:
                row = mine[c:c + 1, :]
            elif c < 0:
                row = halo[0, AGGS + c:AGGS + c + 1, :]
            else:
                row = halo[1, c - AGGS:c - AGGS + 1, :]
            if scale_by is not None:
                row = row / scale_by
            total = total + co[k + 1, s] * row
        return total

    def summed(total):
        return jnp.sum(total.T, axis=0, keepdims=True)

    own2[...] = jnp.zeros_like(own2)
    xrb[...] = jnp.zeros_like(xrb)

    def first_sweep(k):
        rhs = own[k:k + 1, :]
        x1 = rhs / center
        residual = rhs - summed(products(k, own, halo_x, center, True, True))
        x2 = x1 + old_weight * x1 + resid_weight * residual
        own2[k:k + 1, :] = x2
        xrb[k, 0:1, :] = x2

    first_sweep(1)
    first_sweep(2)
    receive_partial(sent[2, 0], 2, 0)
    first_sweep(3)
    receive_partial(sent[2, 1], 2, 1)
    first_sweep(0)
    x2_next = to_neighbour(18, own2, halo_x2.at[0], nxt)
    x2_prev = to_neighbour(19, own2, halo_x2.at[1], prv)
    x2_next.start()
    x2_prev.start()
    pack(3, range(*CUTS[2]))
    pack(0, range(*CUTS[2]))
    repartition(2)
    for off in order + (0,):
        ss[off] = sb[owned((g + off) % groups)]
        if off:
            to_owner(off, *scales).start()
    own_q = pltpu.make_async_copy(sq.at[0], q_out.at[g], self_sem.at[0])
    own_s = pltpu.make_async_copy(ss.at[0], sc_out.at[g], self_sem.at[1])
    own_q.start()
    own_s.start()
    for k in range(AGGS):
        tot[k] = products(k, own2, halo_x2, None, True, False)
    x2_next.wait_recv()
    x2_prev.wait_recv()
    for k in range(AGGS):
        total = tot[k] + products(k, own2, halo_x2, None, False, True)
        xrb[k, 1:2, :] = own[k:k + 1, :] - summed(total)
    for off in order + (0,):
        sx[off] = xrb[owned((g + off) % groups)]
        if off:
            to_owner(off, *vectors).start()
    own_x = pltpu.make_async_copy(sx.at[0], xr_out.at[g], self_sem.at[2])
    own_x.start()

    for copy in (p_next[1], p_prev[1], x_next, x_prev, x2_next, x2_prev):
        copy.wait_send()
    for copies in sent.values():
        for copy in copies:
            copy.wait_send()
    for off in order:
        for args in (*parts, scales, vectors):
            to_owner(off, *args).wait_send()
            from_maker(off, *args).wait_recv()
    own_q.wait()
    own_s.wait()
    own_x.wait()


def call_kernel(groups, rows_axis, owner, lam_low, lam_high, pc, fc, a, p, rhs):
    hbm = pl.BlockSpec(memory_space=pl.ANY)
    smem = pl.BlockSpec(memory_space=pltpu.SMEM)
    vmem = pl.BlockSpec(memory_space=pltpu.VMEM)
    dma = pltpu.SemaphoreType.DMA
    i16 = jnp.int16
    return pl.pallas_call(
        functools.partial(kernel, groups, rows_axis),
        out_shape=(
            jax.ShapeDtypeStruct((groups, 7, BLK, BLK), i16),
            jax.ShapeDtypeStruct((groups, 8, BLK), F32),
            jax.ShapeDtypeStruct((groups, 8, BLK), F32),
        ),
        in_specs=[smem, smem, smem, hbm, vmem, hbm, hbm, hbm, vmem],
        out_specs=(hbm, hbm, hbm),
        scratch_shapes=[
            pltpu.SMEM((2, 2, BLK), jnp.int32),
            pltpu.VMEM((11, 8, BLK), jnp.int32),
            pltpu.SMEM((11, 8, BLK), jnp.int32),
            pltpu.VMEM((ROWS, 5, BLK, BLK), BF16),
            pltpu.VMEM((2 * ROWS + 1, BLK, BLK), BF16),
            pltpu.VMEM((AGG + 1, BLK, BLK), BF16),
            pltpu.VMEM((2 * AGG + 1, BLK, BLK), BF16),
            pltpu.VMEM((AGG + 1, BLK, BLK), BF16),
            pltpu.VMEM((2 * AGG + 1, BLK, BLK), BF16),
            pltpu.VMEM((ROWS, 3 * BLK, BLK), BF16),
            pltpu.VMEM((ROWS, BLK, 5 * BLK), BF16),
            pltpu.VMEM((AGG, BLK, 3 * BLK), F32),
            pltpu.VMEM((AGG, BLK, 3 * BLK), F32),
            pltpu.VMEM((AGGS + 2, 7, BLK, BLK), F32),
            pltpu.VMEM((AGGS + 1, 7, BLK, BLK), i16),
            pltpu.VMEM((AGGS + 1, 8, BLK), F32),
            pltpu.VMEM((groups, 7, BLK, BLK), i16),
            pltpu.VMEM((groups, 8, BLK), F32),
            pltpu.VMEM((AGGS + 1, 8, BLK), F32),
            pltpu.VMEM((groups, 8, BLK), F32),
            pltpu.VMEM((2, 5, BLK, BLK), i16),
            pltpu.VMEM((2, 3, 8, BLK), F32),
            pltpu.VMEM((2, 5, BLK, BLK), i16),
            pltpu.VMEM((2, 3, 8, BLK), F32),
            pltpu.VMEM((8, BLK), F32),
            pltpu.VMEM((2, 8, BLK), F32),
            pltpu.VMEM((8, BLK), F32),
            pltpu.VMEM((2, 8, BLK), F32),
            pltpu.VMEM((AGGS, BLK, BLK), F32),
            dma((AGGS,)), dma, dma((3,)), dma((20,)), dma((20,)),
            dma((groups,)), dma((groups,)),
            dma((groups,)), dma((groups,)), dma((groups,)), dma((groups,)),
            dma((groups,)), dma((groups,)), dma((groups,)), dma((groups,)),
            dma((3,)),
        ],
        compiler_params=pltpu.CompilerParams(
            collective_id=0, has_side_effects=True, vmem_limit_bytes=56 << 20),
    )(owner, lam_low, lam_high, pc, fc, a, p.reshape(2 * ROWS, BLK, BLK), p, rhs)


def open_slots(groups, rows_axis, owner, q_hbm, scale, xr, out_hbm, x_ref, r_ref, q_v, o_v, in_sem, out_sem):
    g = lax.axis_index("grp")
    r = lax.axis_index("row")

    def arrive(n):
        return pltpu.make_async_copy(q_hbm.at[n], q_v.at[n], in_sem.at[n])

    def leave(n):
        return pltpu.make_async_copy(o_v.at[n], out_hbm.at[n], out_sem.at[n])

    for n in range(groups):
        arrive(n).start()
    for n in range(groups):
        x_ref[n:n + 1, :] = xr[n, 0:1, :]
        r_ref[n:n + 1, :] = xr[n, 1:2, :]

    def step(n, carry):
        first = (n * rows_axis + r) * AGGS
        places = [TRAVEL[0].index(s) for s in range(7)]
        for k in range(1, AGGS):
            mine = owner[first + k] == g
            places = [jnp.where(mine, TRAVEL[k].index(s), places[s]) for s in range(7)]
        arrive(n).wait()
        for s in range(7):
            o_v[n, s] = q_v[n, places[s]].astype(jnp.int32).astype(F32) * scale[n, pl.ds(places[s], 1), :]
        leave(n).start()
        return carry

    lax.fori_loop(0, groups, step, 0)
    for n in range(groups):
        leave(n).wait()


def call_open(groups, rows_axis, owner, q, scale, xr):
    hbm = pl.BlockSpec(memory_space=pl.ANY)
    vmem = pl.BlockSpec(memory_space=pltpu.VMEM)
    return pl.pallas_call(
        functools.partial(open_slots, groups, rows_axis),
        out_shape=(
            jax.ShapeDtypeStruct((groups, 7, BLK, BLK), F32),
            jax.ShapeDtypeStruct((groups, BLK), F32),
            jax.ShapeDtypeStruct((groups, BLK), F32),
        ),
        in_specs=[pl.BlockSpec(memory_space=pltpu.SMEM), hbm, vmem, vmem],
        out_specs=(hbm, vmem, vmem),
        scratch_shapes=[
            pltpu.VMEM((groups, 7, BLK, BLK), jnp.int16),
            pltpu.VMEM((groups, 7, BLK, BLK), F32),
            pltpu.SemaphoreType.DMA((groups,)),
            pltpu.SemaphoreType.DMA((groups,)),
        ],
    )(owner, q, scale, xr)


def per_device(
    fine_cols, fine_blocks, prolong_cols, prolong_blocks, agg_owner, coarse_rhs, lam_low, lam_high
):
    groups = lax.axis_size("grp")
    rows_axis = lax.axis_size("row")
    q, scale, xr = call_kernel(
        groups, rows_axis, agg_owner, lam_low, lam_high, prolong_cols.T, fine_cols.T, fine_blocks, prolong_blocks,
        coarse_rhs)
    return call_open(groups, rows_axis, agg_owner, q, scale, xr)


def solution(mesh):
    return jax.shard_map(
        per_device,
        mesh=mesh,
        in_specs=(
            P(("grp", "row"), None),
            P(("grp", "row"), None, None, None),
            P(),
            P(("grp", "row"), None, None, None),
            P(),
            P(("grp", "row"), None),
            P(),
            P(),
        ),
        out_specs=(
            P(("grp", "row"), None, None, None),
            P(("grp", "row"), None),
            P(("grp", "row"), None),
        ),
        check_vma=False,
    )
```

```python
import functools

import jax
import jax.numpy as jnp
from jax import lax
from jax.experimental import pallas as pl
from jax.experimental.pallas import tpu as pltpu
from jax.sharding import PartitionSpec as P

MESH = pl.DeviceIdType.MESH
BLK = 128
AGG = 10
AGGS = 4
ROWS = AGG * AGGS
F32 = jnp.float32
BF16 = jnp.bfloat16
Q_MAX = 32767.0
TINY = 2.0**-110
TOGETHER = 5
TRAVEL = ((5, 6, 0, 1, 4, 2, 3), (3, 4, 5, 6, 0, 1, 2), (0, 1, 2, 3, 6, 5, 4), (0, 1, 6, 5, 2, 4, 3))
CUTS = ((0, 3), (3, 5), (5, 7))
DOWN = (5, 6, 2, 3, 4)
UP = (0, 1, 4, 2, 3)
PARTS = ((0, 2), (2, 3), (3, 5))


def quantised(block):
    top = jnp.maximum(jnp.max(jnp.abs(block), axis=0, keepdims=True), TINY)
    q = jnp.floor(block * (Q_MAX / top) + 0.5).astype(jnp.int32).astype(jnp.int16)
    return q, top * (1.0 / Q_MAX)


def chebyshev_terms(low, high):
    center = 0.5 * (high + low)
    radius = 0.5 * (high - low)
    sigma_ratio = center / radius
    first_rho = 1.0 / sigma_ratio
    second_rho = 1.0 / (2.0 * sigma_ratio - first_rho)
    return center, second_rho * first_rho, 2.0 * second_rho / radius


def wrapped(x, total):
    x = jnp.where(x > total // 2, x - total, x)
    return jnp.where(x < -(total // 2), x + total, x)


def write_tables(fine_total, coarse_total, first_row, base, fc, pc, skip, tbl):
    row = lax.broadcasted_iota(jnp.int32, (5, ROWS), 1)
    reach = wrapped(fc[...] - (first_row + row), fine_total)
    place = row + AGG + reach
    near = [jnp.zeros((5, ROWS), jnp.int32) for _ in range(2)]
    for p in range(ROWS + 2 * AGG):
        for q in range(2):
            near[q] = jnp.where(place == p, pc[(skip + p) // BLK, q, (skip + p) % BLK], near[q])
    agg = jnp.zeros((5, ROWS), jnp.int32)
    for k in range(1, AGGS):
        agg = agg + jnp.where(row >= k * AGG, 1, 0)
    offset = [wrapped(c - base - agg, coarse_total) + 2 for c in near]

    def pick(o, ok, first, second, none):
        got = jnp.where(ok & (offset[0] == o), first, none)
        return jnp.where(ok & (offset[1] == o), second, got)

    inside = (place >= AGG) & (place < ROWS + AGG)
    mine = 2 * (place - AGG)
    for o in range(5):
        tbl[o, 0:5, 0:ROWS] = pick(o, inside, mine, mine + 1, 2 * ROWS)
    below = (place >= 0) & (place < AGG)
    above = (place >= ROWS + AGG) & (place < ROWS + 2 * AGG)
    high = place - ROWS - AGG
    low_part = jnp.where(below & (offset[0] == 0), place, AGG)
    high_part = jnp.where(above & (offset[1] == 4), high, AGG)
    tbl[5, 0:5, 0:ROWS] = jnp.where(row < 2 * AGG, low_part, high_part)
    for n in range(2):
        from_low = pick(1 + n, below, place, place + AGG, 2 * AGG)
        from_high = pick(2 + n, above, high + AGG, high, 2 * AGG)
        tbl[6 + n, 0:5, 0:ROWS] = jnp.where(row < 2 * AGG, from_low, from_high)
    everywhere = row >= 0
    for t in range(3):
        tbl[8 + t, 0:5, 0:ROWS] = pick(t + 1, everywhere, 2 * row, 2 * row + 1, 2 * ROWS)


def kernel(
    groups, rows_axis,
    owner_hbm, low_hbm, high_hbm, pc_hbm, fc_hbm, a_hbm, p_hbm, p_pairs, rhs_hbm,
    q_out, sc_out, xr_out,
    owner, lam_low, lam_high, fc, rhs_v, small_sem, pc, tbl_v, tbl, a_v, p_v, lo_part, lo_all, hi_part, hi_all, pt, m_v, acc_lo, acc_hi, co, qb, sb, sq, ss, xrb, sx,
    pq_s, ps_s, pq_r, ps_r, own, halo_x, own2, halo_x2, tot,
    a_sem, p_sem, t_sem, nb_send, nb_recv, g0_send, g0_recv, g1_send, g1_recv, g2_send, g2_recv,
    gs_send, gs_recv, gx_send, gx_recv, self_sem,
):
    g = lax.axis_index("grp")
    r = lax.axis_index("row")
    device = g * rows_axis + r
    devices = groups * rows_axis
    base = device * AGGS
    last = (r + 1) // rows_axis
    nxt = ((g + last) % groups, (r + 1) % rows_axis)
    first = (rows_axis - r) // rows_axis
    prv = ((g + groups - first) % groups, (r + rows_axis - 1) % rows_axis)

    barrier = pltpu.get_barrier_semaphore()
    for target in (nxt, prv):
        pl.semaphore_signal(barrier, inc=1, device_id=target, device_id_type=MESH)
    for off in range(1, groups):
        pl.semaphore_signal(barrier, inc=1, device_id=((g + off) % groups, r), device_id_type=MESH)

    fine_total = ROWS * devices
    start = (device * ROWS + fine_total - AGG) % fine_total
    chunk = start // BLK
    pc_copies = [
        pltpu.make_async_copy(
            pc_hbm.at[:, pl.ds(pl.multiple_of(((chunk + n) % (fine_total // BLK)) * BLK, BLK), BLK)], pc.at[n], t_sem.at[n])
        for n in range(2)
    ]
    small = [
        pltpu.make_async_copy(src, dst, small_sem.at[n])
        for n, (src, dst) in enumerate(
            ((rhs_hbm, rhs_v), (fc_hbm, fc), (owner_hbm, owner), (low_hbm, lam_low), (high_hbm, lam_high)))
    ]
    for copy in (*pc_copies, *small):
        copy.start()
    p_copy = pltpu.make_async_copy(p_hbm, p_v.at[pl.ds(0, 2 * ROWS)], p_sem)
    p_copy.start()
    a_copies = [
        pltpu.make_async_copy(a_hbm.at[pl.ds(k * AGG, AGG)], a_v.at[pl.ds(k * AGG, AGG)], a_sem.at[k])
        for k in range(AGGS)
    ]
    for k in (0, 3, 1, 2):
        a_copies[k].start()

    tbl_v[...] = jnp.zeros_like(tbl_v)
    pl.semaphore_wait(barrier, groups + 1)

    def to_neighbour(slot, src, dst, target):
        return pltpu.make_async_remote_copy(
            src_ref=src, dst_ref=dst, send_sem=nb_send.at[slot], recv_sem=nb_recv.at[slot],
            device_id=target, device_id_type=MESH)

    last_rows = pl.ds(ROWS - AGG, AGG)
    first_rows = pl.ds(0, AGG)
    rest = pl.ds(AGG, AGG)
    p_next = (
        to_neighbour(0, p_pairs.at[last_rows, 0], lo_part.at[first_rows], nxt),
        to_neighbour(1, p_pairs.at[last_rows, 1], lo_all.at[rest], nxt),
    )
    p_prev = (
        to_neighbour(2, p_pairs.at[first_rows, 1], hi_part.at[first_rows], prv),
        to_neighbour(3, p_pairs.at[first_rows, 0], hi_all.at[rest], prv),
    )
    p_next[0].start()
    p_prev[0].start()
    small[0].wait()
    own[...] = jnp.zeros_like(own)
    own[0:AGGS, :] = rhs_v[...]
    x_next = to_neighbour(4, own, halo_x.at[0], nxt)
    x_prev = to_neighbour(5, own, halo_x.at[1], prv)
    x_next.start()
    x_prev.start()

    for copy in (*pc_copies, *small[1:]):
        copy.wait()
    write_tables(fine_total, AGGS * devices, device * ROWS, base, fc, pc, start % BLK, tbl_v)
    t_copy = pltpu.make_async_copy(tbl_v, tbl, t_sem.at[2])
    t_copy.start()
    zero_block = jnp.zeros((BLK, BLK), BF16)
    p_v[2 * ROWS] = zero_block
    pt[2 * ROWS] = zero_block
    lo_part[AGG] = zero_block
    hi_part[AGG] = zero_block
    lo_all[2 * AGG] = zero_block
    hi_all[2 * AGG] = zero_block
    co[...] = jnp.zeros_like(co)
    t_copy.wait()
    p_copy.wait()

    def for_rows(count, body):
        def step(n, carry):
            for m in range(TOGETHER):
                body(n * TOGETHER + m)
            return carry

        lax.fori_loop(0, count // TOGETHER, step, 0)

    def turn(i):
        for q in range(2):
            pt[2 * i + q] = p_v[2 * i + q].T

    for_rows(ROWS, turn)

    def gathered(ref, i, plane, entries, cols):
        return jnp.concatenate(
            [jnp.concatenate([ref[tbl[plane + o, a, i]] for o in cols], axis=1) for a in entries], axis=0)

    def local_rows(start, count, plan):
        def body(n):
            i = start + n
            lhs = jnp.concatenate([a_v[i, a] for a in range(5)], axis=1)
            for cols, keep, first_col in plan:
                got = jnp.dot(lhs, gathered(p_v, i, 0, range(5), cols), preferred_element_type=F32)
                lo = (cols[0] - first_col) * BLK
                hi = (cols[-1] + 1 - first_col) * BLK
                if keep is None:
                    m_v[i, :, lo:hi] = got.astype(BF16)
                else:
                    keep[n, :, lo:hi] = got

        for_rows(count, body)

    def lift(k, groups_of_cols):
        lhs = jnp.concatenate(
            [jnp.concatenate([pt[tbl[8 + t, 0, k * AGG + n]] for n in range(AGG)], axis=1) for t in range(3)], axis=0)
        for cols in groups_of_cols:
            rhs = m_v[k * AGG:(k + 1) * AGG, :, cols[0] * BLK:(cols[-1] + 1) * BLK]
            rhs = rhs.reshape(AGG * BLK, len(cols) * BLK)
            got = jnp.dot(lhs, rhs, preferred_element_type=F32)
            for t in range(3):
                for n, o in enumerate(cols):
                    co[k + t, o - t + 2] += got[t * BLK:(t + 1) * BLK, n * BLK:(n + 1) * BLK]

    def send_partial(part, side):
        row, all_s, target = ((0, DOWN, prv), (AGGS + 1, UP, nxt))[side]
        lo, hi = PARTS[part]
        ps_s[side, part] = jnp.zeros_like(ps_s[side, part])
        for n in range(lo, hi):
            q, scale = quantised(co[row, all_s[n]])
            pq_s[side, n] = q
            ps_s[side, part, n:n + 1, :] = scale
        slot = 6 + 4 * part + 2 * side
        copies = (
            to_neighbour(slot, pq_s.at[side, pl.ds(lo, hi - lo)], pq_r.at[side, pl.ds(lo, hi - lo)], target),
            to_neighbour(slot + 1, ps_s.at[side, part], ps_r.at[side, part], target),
        )
        for copy in copies:
            copy.start()
        return copies

    def receive_partial(copies, part, side):
        row, all_s = ((AGGS, DOWN), (1, UP))[side]
        for copy in copies:
            copy.wait_recv()
        for n in range(*PARTS[part]):
            co[row, all_s[n]] += pq_r[side, n].astype(jnp.int32).astype(F32) * ps_r[side, part, n:n + 1, :]

    a_copies[0].wait()
    local_rows(0, AGG, (((3, 4), None, 0),))
    lift(0, ((3, 4),))
    sent = {(0, 0): send_partial(0, 0)}
    a_copies[3].wait()
    local_rows(3 * AGG, AGG, (((0, 1), None, 0),))
    lift(3, ((0, 1),))
    sent[0, 1] = send_partial(0, 1)
    inner = (((0, 1), None, 0), ((2, 3), None, 0), ((4,), None, 0))
    a_copies[1].wait()
    local_rows(AGG, AGG, inner)
    p_next[0].wait_send()
    p_next[1].start()
    p_prev[0].wait_send()
    p_prev[1].start()
    a_copies[2].wait()
    local_rows(2 * AGG, AGG, inner)
    lift(1, ((0, 1), (2, 3), (4,)))
    lift(2, ((0, 1), (2, 3), (4,)))

    def pack(k, places):
        for place in places:
            q, scale = quantised(co[k + 1, TRAVEL[k][place]])
            qb[k, place] = q
            sb[k, place:place + 1, :] = scale

    def owned(dest):
        k = AGGS
        for c in range(AGGS):
            k = jnp.where(owner[base + c] == dest, c, k)
        return k

    def to_owner(off, src, dst, send, recv, lo, hi):
        return pltpu.make_async_remote_copy(
            src_ref=src.at[off, pl.ds(lo, hi - lo)], dst_ref=dst.at[g, pl.ds(lo, hi - lo)],
            send_sem=send.at[off], recv_sem=recv.at[off],
            device_id=((g + off) % groups, r), device_id_type=MESH)

    def from_maker(off, src, dst, send, recv, lo, hi):
        return pltpu.make_async_remote_copy(
            src_ref=src.at[off, pl.ds(lo, hi - lo)],
            dst_ref=dst.at[(g + groups - off) % groups, pl.ds(lo, hi - lo)], send_sem=send.at[off],
            recv_sem=recv.at[off], device_id=((g + groups - off) % groups, r), device_id_type=MESH)

    order = (4, 3, 5, 2, 6, 1, 7)
    parts = (
        (sq, q_out, g0_send, g0_recv, *CUTS[0]),
        (sq, q_out, g1_send, g1_recv, *CUTS[1]),
        (sq, q_out, g2_send, g2_recv, *CUTS[2]),
    )
    scales = (ss, sc_out, gs_send, gs_recv, 0, 8)
    vectors = (sx, xr_out, gx_send, gx_recv, 0, 8)

    def repartition(part):
        lo, hi = CUTS[part]
        for off in order + (0,):
            sq[off, lo:hi] = qb[owned((g + off) % groups), lo:hi]
            if off:
                to_owner(off, *parts[part]).start()

    qb[AGGS] = jnp.zeros_like(qb[AGGS])
    sb[...] = jnp.zeros_like(sb)
    for side in range(2):
        receive_partial(sent[0, side], 0, side)
    for k in range(AGGS):
        pack(k, range(*CUTS[0]))
    repartition(0)
    local_rows(0, AGG, (((0, 1), acc_lo, 0), ((2,), acc_lo, 0)))
    local_rows(3 * AGG, AGG, (((2, 3), acc_hi, 2), ((4,), acc_hi, 2)))

    def halo_rows(start, ref, plane, count, keep, keep_col, first_col):
        width = count * BLK

        def body(n):
            i = start + n
            lhs = jnp.concatenate([a_v[i, a] for a in range(1, 5)], axis=1)
            got = jnp.dot(lhs, gathered(ref, i, plane, range(1, 5), range(count)), preferred_element_type=F32)
            got = got + keep[n, :, keep_col * BLK:keep_col * BLK + width]
            m_v[i, :, first_col * BLK:first_col * BLK + width] = got.astype(BF16)

        for_rows(AGG, body)

    p_next[0].wait_recv()
    halo_rows(0, lo_part, 5, 1, acc_lo, 0, 0)
    lift(0, ((0,),))
    sent[1, 0] = send_partial(1, 0)
    p_prev[0].wait_recv()
    halo_rows(3 * AGG, hi_part, 5, 1, acc_hi, 2, 4)
    lift(3, ((4,),))
    sent[1, 1] = send_partial(1, 1)
    lo_all[0:AGG] = lo_part[0:AGG]
    hi_all[0:AGG] = hi_part[0:AGG]
    p_next[1].wait_recv()
    halo_rows(0, lo_all, 6, 2, acc_lo, 1, 1)
    lift(0, ((1, 2),))
    sent[2, 0] = send_partial(2, 0)
    p_prev[1].wait_recv()
    halo_rows(3 * AGG, hi_all, 6, 2, acc_hi, 0, 2)
    lift(3, ((2, 3),))
    sent[2, 1] = send_partial(2, 1)

    for side in range(2):
        receive_partial(sent[1, side], 1, side)
    for k in range(AGGS):
        pack(k, range(*CUTS[1]))
    repartition(1)
    pack(1, range(*CUTS[2]))
    pack(2, range(*CUTS[2]))

    x_next.wait_recv()
    x_prev.wait_recv()
    center, old_weight, resid_weight = chebyshev_terms(
        jnp.full((1, BLK), lam_low[0], F32), jnp.full((1, BLK), lam_high[0], F32))

    def products(k, mine, halo, scale_by, of_mine, of_halo):
        total = jnp.zeros((BLK, BLK), F32)
        for s in range(7):
            c = k + s - 3
            here = 0 <= c < AGGS
            if not (of_mine if here else of_halo):
                continue
            if here:
                row = mine[c:c + 1, :]
            elif c < 0:
                row = halo[0, AGGS + c:AGGS + c + 1, :]
            else:
                row = halo[1, c - AGGS:c - AGGS + 1, :]
            if scale_by is not None:
                row = row / scale_by
            total = total + co[k + 1, s] * row
        return total

    def summed(total):
        return jnp.sum(total.T, axis=0, keepdims=True)

    own2[...] = jnp.zeros_like(own2)
    xrb[...] = jnp.zeros_like(xrb)

    def first_sweep(k):
        rhs = own[k:k + 1, :]
        x1 = rhs / center
        residual = rhs - summed(products(k, own, halo_x, center, True, True))
        x2 = x1 + old_weight * x1 + resid_weight * residual
        own2[k:k + 1, :] = x2
        xrb[k, 0:1, :] = x2

    first_sweep(1)
    first_sweep(2)
    receive_partial(sent[2, 0], 2, 0)
    first_sweep(3)
    receive_partial(sent[2, 1], 2, 1)
    first_sweep(0)
    x2_next = to_neighbour(18, own2, halo_x2.at[0], nxt)
    x2_prev = to_neighbour(19, own2, halo_x2.at[1], prv)
    x2_next.start()
    x2_prev.start()
    pack(3, range(*CUTS[2]))
    pack(0, range(*CUTS[2]))
    repartition(2)
    for off in order + (0,):
        ss[off] = sb[owned((g + off) % groups)]
        if off:
            to_owner(off, *scales).start()
    own_q = pltpu.make_async_copy(sq.at[0], q_out.at[g], self_sem.at[0])
    own_s = pltpu.make_async_copy(ss.at[0], sc_out.at[g], self_sem.at[1])
    own_q.start()
    own_s.start()
    for k in range(AGGS):
        tot[k] = products(k, own2, halo_x2, None, True, False)
    x2_next.wait_recv()
    x2_prev.wait_recv()
    for k in range(AGGS):
        total = tot[k] + products(k, own2, halo_x2, None, False, True)
        xrb[k, 1:2, :] = own[k:k + 1, :] - summed(total)
    for off in order + (0,):
        sx[off] = xrb[owned((g + off) % groups)]
        if off:
            to_owner(off, *vectors).start()
    own_x = pltpu.make_async_copy(sx.at[0], xr_out.at[g], self_sem.at[2])
    own_x.start()

    for copy in (p_next[1], p_prev[1], x_next, x_prev, x2_next, x2_prev):
        copy.wait_send()
    for copies in sent.values():
        for copy in copies:
            copy.wait_send()
    for off in order:
        for args in (*parts, scales, vectors):
            to_owner(off, *args).wait_send()
            from_maker(off, *args).wait_recv()
    own_q.wait()
    own_s.wait()
    own_x.wait()


def call_kernel(groups, rows_axis, owner, lam_low, lam_high, pc, fc, a, p, rhs):
    hbm = pl.BlockSpec(memory_space=pl.ANY)
    dma = pltpu.SemaphoreType.DMA
    i16 = jnp.int16
    return pl.pallas_call(
        functools.partial(kernel, groups, rows_axis),
        out_shape=(
            jax.ShapeDtypeStruct((groups, 7, BLK, BLK), i16),
            jax.ShapeDtypeStruct((groups, 8, BLK), F32),
            jax.ShapeDtypeStruct((groups, 8, BLK), F32),
        ),
        in_specs=[hbm] * 9,
        out_specs=(hbm, hbm, hbm),
        scratch_shapes=[
            pltpu.SMEM(owner.shape, jnp.int32),
            pltpu.SMEM((1,), F32),
            pltpu.SMEM((1,), F32),
            pltpu.VMEM((5, ROWS), jnp.int32),
            pltpu.VMEM((AGGS, BLK), F32),
            dma((5,)),
            pltpu.SMEM((2, 2, BLK), jnp.int32),
            pltpu.VMEM((11, 8, BLK), jnp.int32),
            pltpu.SMEM((11, 8, BLK), jnp.int32),
            pltpu.VMEM((ROWS, 5, BLK, BLK), BF16),
            pltpu.VMEM((2 * ROWS + 1, BLK, BLK), BF16),
            pltpu.VMEM((AGG + 1, BLK, BLK), BF16),
            pltpu.VMEM((2 * AGG + 1, BLK, BLK), BF16),
            pltpu.VMEM((AGG + 1, BLK, BLK), BF16),
            pltpu.VMEM((2 * AGG + 1, BLK, BLK), BF16),
            pltpu.VMEM((2 * ROWS + 1, BLK, BLK), BF16),
            pltpu.VMEM((ROWS, BLK, 5 * BLK), BF16),
            pltpu.VMEM((AGG, BLK, 3 * BLK), F32),
            pltpu.VMEM((AGG, BLK, 3 * BLK), F32),
            pltpu.VMEM((AGGS + 2, 7, BLK, BLK), F32),
            pltpu.VMEM((AGGS + 1, 7, BLK, BLK), i16),
            pltpu.VMEM((AGGS + 1, 8, BLK), F32),
            pltpu.VMEM((groups, 7, BLK, BLK), i16),
            pltpu.VMEM((groups, 8, BLK), F32),
            pltpu.VMEM((AGGS + 1, 8, BLK), F32),
            pltpu.VMEM((groups, 8, BLK), F32),
            pltpu.VMEM((2, 5, BLK, BLK), i16),
            pltpu.VMEM((2, 3, 8, BLK), F32),
            pltpu.VMEM((2, 5, BLK, BLK), i16),
            pltpu.VMEM((2, 3, 8, BLK), F32),
            pltpu.VMEM((8, BLK), F32),
            pltpu.VMEM((2, 8, BLK), F32),
            pltpu.VMEM((8, BLK), F32),
            pltpu.VMEM((2, 8, BLK), F32),
            pltpu.VMEM((AGGS, BLK, BLK), F32),
            dma((AGGS,)), dma, dma((3,)), dma((20,)), dma((20,)),
            dma((groups,)), dma((groups,)),
            dma((groups,)), dma((groups,)), dma((groups,)), dma((groups,)),
            dma((groups,)), dma((groups,)), dma((groups,)), dma((groups,)),
            dma((3,)),
        ],
        compiler_params=pltpu.CompilerParams(
            collective_id=0, has_side_effects=True, vmem_limit_bytes=56 << 20),
    )(owner, lam_low, lam_high, pc, fc, a, p.reshape(2 * ROWS, BLK, BLK), p, rhs)


def open_slots(groups, rows_axis, owner, q_hbm, scale, xr, out_hbm, x_ref, r_ref, q_v, o_v, in_sem, out_sem):
    g = lax.axis_index("grp")
    r = lax.axis_index("row")

    def arrive(n):
        return pltpu.make_async_copy(q_hbm.at[n], q_v.at[n], in_sem.at[n])

    def leave(n):
        return pltpu.make_async_copy(o_v.at[n], out_hbm.at[n], out_sem.at[n])

    for n in range(groups):
        arrive(n).start()
    for n in range(groups):
        x_ref[n:n + 1, :] = xr[n, 0:1, :]
        r_ref[n:n + 1, :] = xr[n, 1:2, :]

    def step(n, carry):
        first = (n * rows_axis + r) * AGGS
        places = [TRAVEL[0].index(s) for s in range(7)]
        for k in range(1, AGGS):
            mine = owner[first + k] == g
            places = [jnp.where(mine, TRAVEL[k].index(s), places[s]) for s in range(7)]
        arrive(n).wait()
        for s in range(7):
            o_v[n, s] = q_v[n, places[s]].astype(jnp.int32).astype(F32) * scale[n, pl.ds(places[s], 1), :]
        leave(n).start()
        return carry

    lax.fori_loop(0, groups, step, 0)
    for n in range(groups):
        leave(n).wait()


def call_open(groups, rows_axis, owner, q, scale, xr):
    hbm = pl.BlockSpec(memory_space=pl.ANY)
    vmem = pl.BlockSpec(memory_space=pltpu.VMEM)
    return pl.pallas_call(
        functools.partial(open_slots, groups, rows_axis),
        out_shape=(
            jax.ShapeDtypeStruct((groups, 7, BLK, BLK), F32),
            jax.ShapeDtypeStruct((groups, BLK), F32),
            jax.ShapeDtypeStruct((groups, BLK), F32),
        ),
        in_specs=[pl.BlockSpec(memory_space=pltpu.SMEM), hbm, vmem, vmem],
        out_specs=(hbm, vmem, vmem),
        scratch_shapes=[
            pltpu.VMEM((groups, 7, BLK, BLK), jnp.int16),
            pltpu.VMEM((groups, 7, BLK, BLK), F32),
            pltpu.SemaphoreType.DMA((groups,)),
            pltpu.SemaphoreType.DMA((groups,)),
        ],
    )(owner, q, scale, xr)


def per_device(
    fine_cols, fine_blocks, prolong_cols, prolong_blocks, agg_owner, coarse_rhs, lam_low, lam_high
):
    groups = lax.axis_size("grp")
    rows_axis = lax.axis_size("row")
    q, scale, xr = call_kernel(
        groups, rows_axis, agg_owner, lam_low, lam_high, prolong_cols.T, fine_cols.T, fine_blocks, prolong_blocks,
        coarse_rhs)
    return call_open(groups, rows_axis, agg_owner, q, scale, xr)


def solution(mesh):
    return jax.shard_map(
        per_device,
        mesh=mesh,
        in_specs=(
            P(("grp", "row"), None),
            P(("grp", "row"), None, None, None),
            P(),
            P(("grp", "row"), None, None, None),
            P(),
            P(("grp", "row"), None),
            P(),
            P(),
        ),
        out_specs=(
            P(("grp", "row"), None, None, None),
            P(("grp", "row"), None),
            P(("grp", "row"), None),
        ),
        check_vma=False,
    )
```

```python
import functools

import jax
import jax.numpy as jnp
from jax import lax
from jax.experimental import pallas as pl
from jax.experimental.pallas import tpu as pltpu
from jax.sharding import PartitionSpec as P

MESH = pl.DeviceIdType.MESH
BLK = 128
AGG = 10
AGGS = 4
ROWS = AGG * AGGS
F32 = jnp.float32
BF16 = jnp.bfloat16
Q_MAX = 32767.0
TINY = 2.0**-110
TOGETHER = 5
TRAVEL = ((5, 6, 0, 1, 4, 2, 3), (3, 4, 5, 6, 0, 1, 2), (0, 1, 2, 3, 6, 5, 4), (0, 1, 6, 5, 2, 4, 3))
CUTS = ((0, 3), (3, 5), (5, 7))
DOWN = (5, 6, 2, 3, 4)
UP = (0, 1, 4, 2, 3)
PARTS = ((0, 2), (2, 3), (3, 5))


def quantised(block):
    top = jnp.maximum(jnp.max(jnp.abs(block), axis=0, keepdims=True), TINY)
    q = jnp.floor(block * (Q_MAX / top) + 0.5).astype(jnp.int32).astype(jnp.int16)
    return q, top * (1.0 / Q_MAX)


def chebyshev_terms(low, high):
    center = 0.5 * (high + low)
    radius = 0.5 * (high - low)
    sigma_ratio = center / radius
    first_rho = 1.0 / sigma_ratio
    second_rho = 1.0 / (2.0 * sigma_ratio - first_rho)
    return center, second_rho * first_rho, 2.0 * second_rho / radius


def wrapped(x, total):
    x = jnp.where(x > total // 2, x - total, x)
    return jnp.where(x < -(total // 2), x + total, x)


def write_tables(fine_total, coarse_total, first_row, base, fc, pc, skip, tbl):
    row = lax.broadcasted_iota(jnp.int32, (5, ROWS), 1)
    reach = wrapped(fc[...] - (first_row + row), fine_total)
    place = row + AGG + reach
    near = [jnp.zeros((5, ROWS), jnp.int32) for _ in range(2)]
    for p in range(ROWS + 2 * AGG):
        for q in range(2):
            near[q] = jnp.where(place == p, pc[(skip + p) // BLK, q, (skip + p) % BLK], near[q])
    agg = jnp.zeros((5, ROWS), jnp.int32)
    for k in range(1, AGGS):
        agg = agg + jnp.where(row >= k * AGG, 1, 0)
    offset = [wrapped(c - base - agg, coarse_total) + 2 for c in near]

    def pick(o, ok, first, second, none):
        got = jnp.where(ok & (offset[0] == o), first, none)
        return jnp.where(ok & (offset[1] == o), second, got)

    inside = (place >= AGG) & (place < ROWS + AGG)
    mine = 2 * (place - AGG)
    for o in range(5):
        tbl[o, 0:5, 0:ROWS] = pick(o, inside, mine, mine + 1, 2 * ROWS)
    below = (place >= 0) & (place < AGG)
    above = (place >= ROWS + AGG) & (place < ROWS + 2 * AGG)
    high = place - ROWS - AGG
    low_part = jnp.where(below & (offset[0] == 0), place, AGG)
    high_part = jnp.where(above & (offset[1] == 4), high, AGG)
    tbl[5, 0:5, 0:ROWS] = jnp.where(row < 2 * AGG, low_part, high_part)
    for n in range(2):
        from_low = pick(1 + n, below, place, place + AGG, 2 * AGG)
        from_high = pick(2 + n, above, high + AGG, high, 2 * AGG)
        tbl[6 + n, 0:5, 0:ROWS] = jnp.where(row < 2 * AGG, from_low, from_high)
    everywhere = row >= 0
    for t in range(3):
        tbl[8 + t, 0:5, 0:ROWS] = pick(t + 1, everywhere, 2 * row, 2 * row + 1, 2 * ROWS)


def kernel(
    groups, rows_axis,
    owner_hbm, low_hbm, high_hbm, pc_hbm, fc_hbm, a_hbm, p_hbm, p_pairs, rhs_hbm,
    q_out, sc_out, xr_out,
    owner, lam_low, lam_high, fc, rhs_v, small_sem, pc, tbl_v, tbl, a_v, p_v, lo_part, lo_all, hi_part, hi_all, pt, m_v, acc_lo, acc_hi, co, qb, sb, sq, ss, xrb, sx,
    pq_s, ps_s, pq_r, ps_r, own, halo_x, own2, halo_x2, tot,
    a_sem, p_sem, t_sem, nb_send, nb_recv, g0_send, g0_recv, g1_send, g1_recv, g2_send, g2_recv,
    gs_send, gs_recv, gx_send, gx_recv, self_sem,
):
    g = lax.axis_index("grp")
    r = lax.axis_index("row")
    device = g * rows_axis + r
    devices = groups * rows_axis
    base = device * AGGS
    last = (r + 1) // rows_axis
    nxt = ((g + last) % groups, (r + 1) % rows_axis)
    first = (rows_axis - r) // rows_axis
    prv = ((g + groups - first) % groups, (r + rows_axis - 1) % rows_axis)

    barrier = pltpu.get_barrier_semaphore()
    for target in (nxt, prv):
        pl.semaphore_signal(barrier, inc=1, device_id=target, device_id_type=MESH)
    for off in range(1, groups):
        pl.semaphore_signal(barrier, inc=1, device_id=((g + off) % groups, r), device_id_type=MESH)

    fine_total = ROWS * devices
    start = (device * ROWS + fine_total - AGG) % fine_total
    chunk = start // BLK
    pc_copies = [
        pltpu.make_async_copy(
            pc_hbm.at[:, pl.ds(pl.multiple_of(((chunk + n) % (fine_total // BLK)) * BLK, BLK), BLK)], pc.at[n], t_sem.at[n])
        for n in range(2)
    ]
    small = [
        pltpu.make_async_copy(src, dst, small_sem.at[n])
        for n, (src, dst) in enumerate(
            ((rhs_hbm, rhs_v), (fc_hbm, fc), (owner_hbm, owner), (low_hbm, lam_low), (high_hbm, lam_high)))
    ]
    for copy in (*pc_copies, *small):
        copy.start()
    p_copy = pltpu.make_async_copy(p_hbm, p_v.at[pl.ds(0, 2 * ROWS)], p_sem)
    p_copy.start()
    a_copies = [
        pltpu.make_async_copy(a_hbm.at[pl.ds(k * AGG, AGG)], a_v.at[pl.ds(k * AGG, AGG)], a_sem.at[k])
        for k in range(AGGS)
    ]
    for k in (0, 3, 1, 2):
        a_copies[k].start()

    tbl_v[...] = jnp.zeros_like(tbl_v)
    pl.semaphore_wait(barrier, groups + 1)

    def to_neighbour(slot, src, dst, target):
        return pltpu.make_async_remote_copy(
            src_ref=src, dst_ref=dst, send_sem=nb_send.at[slot], recv_sem=nb_recv.at[slot],
            device_id=target, device_id_type=MESH)

    last_rows = pl.ds(ROWS - AGG, AGG)
    first_rows = pl.ds(0, AGG)
    rest = pl.ds(AGG, AGG)
    p_next = (
        to_neighbour(0, p_pairs.at[last_rows, 0], lo_part.at[first_rows], nxt),
        to_neighbour(1, p_pairs.at[last_rows, 1], lo_all.at[rest], nxt),
    )
    p_prev = (
        to_neighbour(2, p_pairs.at[first_rows, 1], hi_part.at[first_rows], prv),
        to_neighbour(3, p_pairs.at[first_rows, 0], hi_all.at[rest], prv),
    )
    p_next[0].start()
    p_prev[0].start()
    small[0].wait()
    own[...] = jnp.zeros_like(own)
    own[0:AGGS, :] = rhs_v[...]
    x_next = to_neighbour(4, own, halo_x.at[0], nxt)
    x_prev = to_neighbour(5, own, halo_x.at[1], prv)
    x_next.start()
    x_prev.start()

    for copy in (*pc_copies, *small[1:]):
        copy.wait()
    write_tables(fine_total, AGGS * devices, device * ROWS, base, fc, pc, start % BLK, tbl_v)
    t_copy = pltpu.make_async_copy(tbl_v, tbl, t_sem.at[2])
    t_copy.start()
    zero_block = jnp.zeros((BLK, BLK), BF16)
    p_v[2 * ROWS] = zero_block
    pt[2 * ROWS] = zero_block
    lo_part[AGG] = zero_block
    hi_part[AGG] = zero_block
    lo_all[2 * AGG] = zero_block
    hi_all[2 * AGG] = zero_block
    co[...] = jnp.zeros_like(co)
    t_copy.wait()
    p_copy.wait()

    def for_rows(count, body):
        def step(n, carry):
            for m in range(TOGETHER):
                body(n * TOGETHER + m)
            return carry

        lax.fori_loop(0, count // TOGETHER, step, 0)

    def turn(i):
        for q in range(2):
            pt[2 * i + q] = p_v[2 * i + q].T

    for_rows(ROWS, turn)

    def gathered(ref, i, plane, entries, cols):
        return jnp.concatenate(
            [jnp.concatenate([ref[tbl[plane + o, a, i]] for o in cols], axis=1) for a in entries], axis=0)

    def local_rows(start, count, plan):
        def body(n):
            i = start + n
            lhs = jnp.concatenate([a_v[i, a] for a in range(5)], axis=1)
            for cols, keep, first_col in plan:
                got = jnp.dot(lhs, gathered(p_v, i, 0, range(5), cols), preferred_element_type=F32)
                lo = (cols[0] - first_col) * BLK
                hi = (cols[-1] + 1 - first_col) * BLK
                if keep is None:
                    m_v[i, :, lo:hi] = got.astype(BF16)
                else:
                    keep[n, :, lo:hi] = got

        for_rows(count, body)

    def lift(k, groups_of_cols):
        lhs = jnp.concatenate(
            [jnp.concatenate([pt[tbl[8 + t, 0, k * AGG + n]] for n in range(AGG)], axis=1) for t in range(3)], axis=0)
        for cols in groups_of_cols:
            rhs = m_v[k * AGG:(k + 1) * AGG, :, cols[0] * BLK:(cols[-1] + 1) * BLK]
            rhs = rhs.reshape(AGG * BLK, len(cols) * BLK)
            got = jnp.dot(lhs, rhs, preferred_element_type=F32)
            for t in range(3):
                for n, o in enumerate(cols):
                    co[k + t, o - t + 2] += got[t * BLK:(t + 1) * BLK, n * BLK:(n + 1) * BLK]

    def send_partial(part, side):
        row, all_s, target = ((0, DOWN, prv), (AGGS + 1, UP, nxt))[side]
        lo, hi = PARTS[part]
        ps_s[side, part] = jnp.zeros_like(ps_s[side, part])
        for n in range(lo, hi):
            q, scale = quantised(co[row, all_s[n]])
            pq_s[side, n] = q
            ps_s[side, part, n:n + 1, :] = scale
        slot = 6 + 4 * part + 2 * side
        copies = (
            to_neighbour(slot, pq_s.at[side, pl.ds(lo, hi - lo)], pq_r.at[side, pl.ds(lo, hi - lo)], target),
            to_neighbour(slot + 1, ps_s.at[side, part], ps_r.at[side, part], target),
        )
        for copy in copies:
            copy.start()
        return copies

    def receive_partial(copies, part, side):
        row, all_s = ((AGGS, DOWN), (1, UP))[side]
        for copy in copies:
            copy.wait_recv()
        for n in range(*PARTS[part]):
            co[row, all_s[n]] += pq_r[side, n].astype(jnp.int32).astype(F32) * ps_r[side, part, n:n + 1, :]

    a_copies[0].wait()
    local_rows(0, AGG, (((3, 4), None, 0),))
    lift(0, ((3, 4),))
    sent = {(0, 0): send_partial(0, 0)}
    a_copies[3].wait()
    local_rows(3 * AGG, AGG, (((0, 1), None, 0),))
    lift(3, ((0, 1),))
    sent[0, 1] = send_partial(0, 1)
    inner = (((0, 1), None, 0), ((2, 3), None, 0), ((4,), None, 0))
    a_copies[1].wait()
    local_rows(AGG, AGG, inner)
    p_next[0].wait_send()
    p_next[1].start()
    p_prev[0].wait_send()
    p_prev[1].start()
    a_copies[2].wait()
    local_rows(2 * AGG, AGG, inner)
    lift(1, ((0, 1), (2, 3), (4,)))
    lift(2, ((0, 1), (2, 3), (4,)))

    def pack(k, places):
        for place in places:
            q, scale = quantised(co[k + 1, TRAVEL[k][place]])
            qb[k, place] = q
            sb[k, place:place + 1, :] = scale

    def owned(dest):
        k = AGGS
        for c in range(AGGS):
            k = jnp.where(owner[base + c] == dest, c, k)
        return k

    def to_owner(off, src, dst, send, recv, lo, hi):
        return pltpu.make_async_remote_copy(
            src_ref=src.at[off, pl.ds(lo, hi - lo)], dst_ref=dst.at[g, pl.ds(lo, hi - lo)],
            send_sem=send.at[off], recv_sem=recv.at[off],
            device_id=((g + off) % groups, r), device_id_type=MESH)

    def from_maker(off, src, dst, send, recv, lo, hi):
        return pltpu.make_async_remote_copy(
            src_ref=src.at[off, pl.ds(lo, hi - lo)],
            dst_ref=dst.at[(g + groups - off) % groups, pl.ds(lo, hi - lo)], send_sem=send.at[off],
            recv_sem=recv.at[off], device_id=((g + groups - off) % groups, r), device_id_type=MESH)

    order = (4, 3, 5, 2, 6, 1, 7)
    parts = (
        (sq, q_out, g0_send, g0_recv, *CUTS[0]),
        (sq, q_out, g1_send, g1_recv, *CUTS[1]),
        (sq, q_out, g2_send, g2_recv, *CUTS[2]),
    )
    scales = (ss, sc_out, gs_send, gs_recv, 0, 8)
    vectors = (sx, xr_out, gx_send, gx_recv, 0, 8)

    def repartition(part):
        lo, hi = CUTS[part]
        for off in order + (0,):
            sq[off, lo:hi] = qb[owned((g + off) % groups), lo:hi]
            if off:
                to_owner(off, *parts[part]).start()

    qb[AGGS] = jnp.zeros_like(qb[AGGS])
    sb[...] = jnp.zeros_like(sb)
    for side in range(2):
        receive_partial(sent[0, side], 0, side)
    for k in range(AGGS):
        pack(k, range(*CUTS[0]))
    repartition(0)
    local_rows(0, AGG, (((0, 1), acc_lo, 0), ((2,), acc_lo, 0)))
    local_rows(3 * AGG, AGG, (((2, 3), acc_hi, 2), ((4,), acc_hi, 2)))

    def halo_rows(start, ref, plane, count, keep, keep_col, first_col):
        width = count * BLK

        def body(n):
            i = start + n
            lhs = jnp.concatenate([a_v[i, a] for a in range(1, 5)], axis=1)
            got = jnp.dot(lhs, gathered(ref, i, plane, range(1, 5), range(count)), preferred_element_type=F32)
            got = got + keep[n, :, keep_col * BLK:keep_col * BLK + width]
            m_v[i, :, first_col * BLK:first_col * BLK + width] = got.astype(BF16)

        for_rows(AGG, body)

    p_next[0].wait_recv()
    halo_rows(0, lo_part, 5, 1, acc_lo, 0, 0)
    lift(0, ((0,),))
    sent[1, 0] = send_partial(1, 0)
    p_prev[0].wait_recv()
    halo_rows(3 * AGG, hi_part, 5, 1, acc_hi, 2, 4)
    lift(3, ((4,),))
    sent[1, 1] = send_partial(1, 1)
    lo_all[0:AGG] = lo_part[0:AGG]
    hi_all[0:AGG] = hi_part[0:AGG]
    p_next[1].wait_recv()
    halo_rows(0, lo_all, 6, 2, acc_lo, 1, 1)
    lift(0, ((1, 2),))
    sent[2, 0] = send_partial(2, 0)
    p_prev[1].wait_recv()
    halo_rows(3 * AGG, hi_all, 6, 2, acc_hi, 0, 2)
    lift(3, ((2, 3),))
    sent[2, 1] = send_partial(2, 1)

    for side in range(2):
        receive_partial(sent[1, side], 1, side)
    for k in range(AGGS):
        pack(k, range(*CUTS[1]))
    repartition(1)
    pack(1, range(*CUTS[2]))
    pack(2, range(*CUTS[2]))

    x_next.wait_recv()
    x_prev.wait_recv()
    center, old_weight, resid_weight = chebyshev_terms(
        jnp.full((1, BLK), lam_low[0], F32), jnp.full((1, BLK), lam_high[0], F32))

    def products(k, mine, halo, scale_by, of_mine, of_halo):
        total = jnp.zeros((BLK, BLK), F32)
        for s in range(7):
            c = k + s - 3
            here = 0 <= c < AGGS
            if not (of_mine if here else of_halo):
                continue
            if here:
                row = mine[c:c + 1, :]
            elif c < 0:
                row = halo[0, AGGS + c:AGGS + c + 1, :]
            else:
                row = halo[1, c - AGGS:c - AGGS + 1, :]
            if scale_by is not None:
                row = row / scale_by
            total = total + co[k + 1, s] * row
        return total

    def summed(total):
        return jnp.sum(total.T, axis=0, keepdims=True)

    own2[...] = jnp.zeros_like(own2)
    xrb[...] = jnp.zeros_like(xrb)

    def first_sweep(k):
        rhs = own[k:k + 1, :]
        x1 = rhs / center
        residual = rhs - summed(products(k, own, halo_x, center, True, True))
        x2 = x1 + old_weight * x1 + resid_weight * residual
        own2[k:k + 1, :] = x2
        xrb[k, 0:1, :] = x2

    first_sweep(1)
    first_sweep(2)
    receive_partial(sent[2, 0], 2, 0)
    first_sweep(3)
    receive_partial(sent[2, 1], 2, 1)
    first_sweep(0)
    x2_next = to_neighbour(18, own2, halo_x2.at[0], nxt)
    x2_prev = to_neighbour(19, own2, halo_x2.at[1], prv)
    x2_next.start()
    x2_prev.start()
    pack(3, range(*CUTS[2]))
    pack(0, range(*CUTS[2]))
    repartition(2)
    for off in order + (0,):
        ss[off] = sb[owned((g + off) % groups)]
        if off:
            to_owner(off, *scales).start()
    own_q = pltpu.make_async_copy(sq.at[0], q_out.at[g], self_sem.at[0])
    own_s = pltpu.make_async_copy(ss.at[0], sc_out.at[g], self_sem.at[1])
    own_q.start()
    own_s.start()
    for k in range(AGGS):
        tot[k] = products(k, own2, halo_x2, None, True, False)
    x2_next.wait_recv()
    x2_prev.wait_recv()
    for k in range(AGGS):
        total = tot[k] + products(k, own2, halo_x2, None, False, True)
        xrb[k, 1:2, :] = own[k:k + 1, :] - summed(total)
    for off in order + (0,):
        sx[off] = xrb[owned((g + off) % groups)]
        if off:
            to_owner(off, *vectors).start()
    own_x = pltpu.make_async_copy(sx.at[0], xr_out.at[g], self_sem.at[2])
    own_x.start()

    for copy in (p_next[1], p_prev[1], x_next, x_prev, x2_next, x2_prev):
        copy.wait_send()
    for copies in sent.values():
        for copy in copies:
            copy.wait_send()
    for off in order:
        for args in (*parts, scales, vectors):
            to_owner(off, *args).wait_send()
            from_maker(off, *args).wait_recv()
    own_q.wait()
    own_s.wait()
    own_x.wait()


def call_kernel(groups, rows_axis, owner, lam_low, lam_high, pc, fc, a, p, rhs):
    hbm = pl.BlockSpec(memory_space=pl.ANY)
    dma = pltpu.SemaphoreType.DMA
    i16 = jnp.int16
    return pl.pallas_call(
        functools.partial(kernel, groups, rows_axis),
        out_shape=(
            jax.ShapeDtypeStruct((groups, 7, BLK, BLK), i16),
            jax.ShapeDtypeStruct((groups, 8, BLK), F32),
            jax.ShapeDtypeStruct((groups, 8, BLK), F32),
        ),
        in_specs=[hbm] * 9,
        out_specs=(hbm, hbm, hbm),
        scratch_shapes=[
            pltpu.SMEM(owner.shape, jnp.int32),
            pltpu.SMEM((1,), F32),
            pltpu.SMEM((1,), F32),
            pltpu.VMEM((5, ROWS), jnp.int32),
            pltpu.VMEM((AGGS, BLK), F32),
            dma((5,)),
            pltpu.SMEM((2, 2, BLK), jnp.int32),
            pltpu.VMEM((11, 8, BLK), jnp.int32),
            pltpu.SMEM((11, 8, BLK), jnp.int32),
            pltpu.VMEM((ROWS, 5, BLK, BLK), BF16),
            pltpu.VMEM((2 * ROWS + 1, BLK, BLK), BF16),
            pltpu.VMEM((AGG + 1, BLK, BLK), BF16),
            pltpu.VMEM((2 * AGG + 1, BLK, BLK), BF16),
            pltpu.VMEM((AGG + 1, BLK, BLK), BF16),
            pltpu.VMEM((2 * AGG + 1, BLK, BLK), BF16),
            pltpu.VMEM((2 * ROWS + 1, BLK, BLK), BF16),
            pltpu.VMEM((ROWS, BLK, 5 * BLK), BF16),
            pltpu.VMEM((AGG, BLK, 3 * BLK), F32),
            pltpu.VMEM((AGG, BLK, 3 * BLK), F32),
            pltpu.VMEM((AGGS + 2, 7, BLK, BLK), F32),
            pltpu.VMEM((AGGS + 1, 7, BLK, BLK), i16),
            pltpu.VMEM((AGGS + 1, 8, BLK), F32),
            pltpu.VMEM((groups, 7, BLK, BLK), i16),
            pltpu.VMEM((groups, 8, BLK), F32),
            pltpu.VMEM((AGGS + 1, 8, BLK), F32),
            pltpu.VMEM((groups, 8, BLK), F32),
            pltpu.VMEM((2, 5, BLK, BLK), i16),
            pltpu.VMEM((2, 3, 8, BLK), F32),
            pltpu.VMEM((2, 5, BLK, BLK), i16),
            pltpu.VMEM((2, 3, 8, BLK), F32),
            pltpu.VMEM((8, BLK), F32),
            pltpu.VMEM((2, 8, BLK), F32),
            pltpu.VMEM((8, BLK), F32),
            pltpu.VMEM((2, 8, BLK), F32),
            pltpu.VMEM((AGGS, BLK, BLK), F32),
            dma((AGGS,)), dma, dma((3,)), dma((20,)), dma((20,)),
            dma((groups,)), dma((groups,)),
            dma((groups,)), dma((groups,)), dma((groups,)), dma((groups,)),
            dma((groups,)), dma((groups,)), dma((groups,)), dma((groups,)),
            dma((3,)),
        ],
        compiler_params=pltpu.CompilerParams(
            collective_id=0, has_side_effects=True, vmem_limit_bytes=56 << 20),
    )(owner, lam_low, lam_high, pc, fc, a, p.reshape(2 * ROWS, BLK, BLK), p, rhs)


def open_slots(
    groups, rows_axis, owner_hbm, q_hbm, scale_hbm, xr_hbm, out_hbm, x_hbm, r_hbm,
    owner, scale, xr, x_v, r_v, q_v, o_v, in_sem, out_sem, small_sem,
):
    g = lax.axis_index("grp")
    r = lax.axis_index("row")

    def arrive(n):
        return pltpu.make_async_copy(q_hbm.at[n], q_v.at[n], in_sem.at[n])

    def leave(n):
        return pltpu.make_async_copy(o_v.at[n], out_hbm.at[n], out_sem.at[n])

    small = [
        pltpu.make_async_copy(src, dst, small_sem.at[n])
        for n, (src, dst) in enumerate(
            ((owner_hbm, owner), (scale_hbm, scale), (xr_hbm, xr), (x_v, x_hbm), (r_v, r_hbm)))
    ]
    small[0].start()
    small[1].start()
    for n in range(groups):
        arrive(n).start()
    small[2].start()
    small[0].wait()
    small[1].wait()

    def step(n, carry):
        first = (n * rows_axis + r) * AGGS
        places = [TRAVEL[0].index(s) for s in range(7)]
        for k in range(1, AGGS):
            mine = owner[first + k] == g
            places = [jnp.where(mine, TRAVEL[k].index(s), places[s]) for s in range(7)]
        arrive(n).wait()
        for s in range(7):
            o_v[n, s] = q_v[n, places[s]].astype(jnp.int32).astype(F32) * scale[n, pl.ds(places[s], 1), :]
        leave(n).start()
        return carry

    lax.fori_loop(0, groups, step, 0)
    small[2].wait()
    for n in range(groups):
        x_v[n:n + 1, :] = xr[n, 0:1, :]
        r_v[n:n + 1, :] = xr[n, 1:2, :]
    small[3].start()
    small[4].start()
    small[3].wait()
    small[4].wait()
    for n in range(groups):
        leave(n).wait()


def call_open(groups, rows_axis, owner, q, scale, xr):
    hbm = pl.BlockSpec(memory_space=pl.ANY)
    return pl.pallas_call(
        functools.partial(open_slots, groups, rows_axis),
        out_shape=(
            jax.ShapeDtypeStruct((groups, 7, BLK, BLK), F32),
            jax.ShapeDtypeStruct((groups, BLK), F32),
            jax.ShapeDtypeStruct((groups, BLK), F32),
        ),
        in_specs=[hbm] * 4,
        out_specs=(hbm,) * 3,
        scratch_shapes=[
            pltpu.SMEM(owner.shape, jnp.int32),
            pltpu.VMEM((groups, 8, BLK), F32),
            pltpu.VMEM((groups, 8, BLK), F32),
            pltpu.VMEM((groups, BLK), F32),
            pltpu.VMEM((groups, BLK), F32),
            pltpu.VMEM((groups, 7, BLK, BLK), jnp.int16),
            pltpu.VMEM((groups, 7, BLK, BLK), F32),
            pltpu.SemaphoreType.DMA((groups,)),
            pltpu.SemaphoreType.DMA((groups,)),
            pltpu.SemaphoreType.DMA((5,)),
        ],
    )(owner, q, scale, xr)


def per_device(
    fine_cols, fine_blocks, prolong_cols, prolong_blocks, agg_owner, coarse_rhs, lam_low, lam_high
):
    groups = lax.axis_size("grp")
    rows_axis = lax.axis_size("row")
    q, scale, xr = call_kernel(
        groups, rows_axis, agg_owner, lam_low, lam_high, prolong_cols.T, fine_cols.T, fine_blocks, prolong_blocks,
        coarse_rhs)
    return call_open(groups, rows_axis, agg_owner, q, scale, xr)


def solution(mesh):
    return jax.shard_map(
        per_device,
        mesh=mesh,
        in_specs=(
            P(("grp", "row"), None),
            P(("grp", "row"), None, None, None),
            P(),
            P(("grp", "row"), None, None, None),
            P(),
            P(("grp", "row"), None),
            P(),
            P(),
        ),
        out_specs=(
            P(("grp", "row"), None, None, None),
            P(("grp", "row"), None),
            P(("grp", "row"), None),
        ),
        check_vma=False,
    )
```
